256 devices in a mesh: pipe: 8 (over x_lo, y), expert: 32 (over z, x_hi, core).
Axes of the slice: x: 4 (x_hi: 2, x_lo: 2; x = x_hi * 2 + x_lo), y: 4, z: 8, core: 2. Of those that a mesh axis runs over, the one named last changes fastest.
Arguments:
- tokens: bfloat16 [8, 4096, 2048], P('pipe', 'expert'), may hold values from -6 to 6
- routes: int32 [8, 4096, 6], P('pipe', 'expert'), may hold values from 0 to 31, all different within a row; in each aligned block of 128 rows (0 to 127, 128 to 255, ..., all dimensions but the last counted through in order) at most 36 rows name the same one
- norm_gain: float32 [8, 2048], P('pipe'), may hold values from 0.1 to 1.9
- router_weight: bfloat16 [8, 2048, 32], P('pipe'), may hold values from -0.125 to 0.125
- w_gate: bfloat16 [8, 32, 2048, 768], P('pipe', 'expert'), may hold values from -0.125 to 0.125
- w_up: bfloat16 [8, 32, 2048, 768], P('pipe', 'expert'), may hold values from -0.125 to 0.125
- w_down: bfloat16 [8, 32, 768, 2048], P('pipe', 'expert'), may hold values from -0.21875 to 0.21875
Outputs:
- received: bfloat16 [8, 4096, 2048], P('pipe', 'expert')
The draws below stay inside these ranges and needn't reach their ends.
Inputs may be any that keep to these rules, and one draw needn't show every extreme that they name: Within each aligned block of 128 tokens of a section (the tokens of one device), the 6 routes of a token name different experts and no expert is named by more than 36 routes; some expert is named by exactly 36 routes in some block; every expert is named somewhere.
All inputs are finite; a program needn't handle non-finite values.
Results may differ from the reference program's by a relative error of at most 0.0039.
Values may be sent and summed in bfloat16 or wider, within the bound.
A program may use at most 128 MiB of HBM per device.

```python
import math
import jax
import jax.numpy as jnp
import numpy as np
from jax import lax

D = 2048
FF = 768
TOP = 6
TOK_DEV = 128
EXPERTS = 32
SECTIONS = 8
TOKENS = 4096
CAP = 36
N_EXPERT = 32


def levels(rng, dims, cuts, smallest, top_value):
    gain, own = 1.0, jax.random.fold_in(rng, 6)
    for position, blocks in cuts:
        heights = jnp.exp(jax.random.uniform(jax.random.fold_in(own, position), (blocks,), jnp.float32, smallest / len(cuts), top_value / len(cuts)))
        gain = gain * jnp.repeat(heights, dims[position] // blocks).reshape([-1 if axis == position else 1 for axis in range(len(dims))])
    return gain


def routed_block(rng, own, number, rows, amount, top, most, lean):
    order = jax.random.permutation(rng, amount)
    packed, common = shares(amount, rows * top, most, lean, True), shares(amount, rows * top, most, lean, False)
    places = jnp.arange(amount)

    def named(tallies, turn):
        used = int((tallies > 0).sum())
        fixed = max(1, used // 4)
        passed = fixed + (places - fixed + turn * (used - fixed)) % max(1, amount - fixed)
        return jnp.zeros((amount,), jnp.int32).at[order[jnp.where(places < fixed, places, passed)]].set(jnp.asarray(tallies, jnp.int32))

    tallies = jnp.where(number % 4 == 0, named(packed, number // 4), named(common, number - number // 4 - 1))
    mixed = jax.random.permutation(jax.random.fold_in(own, 3), amount)
    giver, sink = mixed[0:amount // 2 * 2:2], mixed[1:amount // 2 * 2:2]
    slack = jnp.minimum(tallies[giver] - 1, most - tallies[sink]) // 2
    slack = jnp.where((giver == order[0]) | (sink == order[0]) | (tallies[sink] == 0), 0, jnp.maximum(slack, 0))
    passed = jax.random.randint(jax.random.fold_in(own, 4), (amount // 2,), 0, 1 << 20) % (slack + 1)
    tallies = tallies.at[giver].add(-passed).at[sink].add(passed)
    items = jnp.searchsorted(jnp.cumsum(tallies), jnp.arange(rows * top), side="right").astype(jnp.int32)
    table = items.reshape(top, rows).T
    table = table[jax.random.permutation(jax.random.fold_in(own, 1), rows)]
    turn = jax.random.randint(jax.random.fold_in(own, 2), (rows, 1), 0, top)
    return jnp.take_along_axis(table, (jnp.arange(top)[None, :] + turn) % top, axis=1)


def shares(amount, total, bound, lean, full):
    loads = [(1 << 20) // math.isqrt(grade ** lean) + 1 for grade in range(1, amount + 1)]
    largest = bound if full else min(bound, max(-(-total // amount), total * loads[0] // sum(loads)))
    least = 1 if total - largest >= amount - 1 else 0
    given, rest = [largest] + [least] * (amount - 1), total - largest - least * (amount - 1)
    while rest > 0:
        candidates = [i for i in range(1, amount) if given[i] < largest] or [i for i in range(1, amount) if given[i] < bound]
        whole, left = sum([loads[i] for i in candidates]), rest
        for i in candidates:
            more = min(bound - given[i], max(1, left * loads[i] // whole), rest)
            given[i] = given[i] + more
            rest = rest - more
    return np.array(given)


def gaussian(key, extent, width, reach, split=(), kind=jnp.bfloat16):
    values = width * jax.random.normal(key, extent, jnp.float32)
    if split:
        values = values * levels(key, extent, split, -0.22, 0.18)
    return jnp.clip(values, -reach, reach).astype(kind)


def setup_inputs(seed: int = 0) -> dict:
    seeds = jax.random.split(jax.random.key(seed), 8)
    tokens = gaussian(seeds[0], (SECTIONS, TOKENS, D), 1.0, 6.0, ((0, 8), (1, 32)))
    routes_keys = jax.random.split(jax.random.fold_in(seeds[1], 1), SECTIONS * TOKENS // TOK_DEV)
    routes_turns = jax.random.permutation(jax.random.fold_in(seeds[1], 3), SECTIONS * TOKENS // TOK_DEV)
    routes = jax.vmap(lambda own, number: routed_block(jax.random.fold_in(seeds[1], 2), own, number, TOK_DEV, EXPERTS, TOP, CAP, 2))(routes_keys, routes_turns).reshape((SECTIONS, TOKENS, TOP))
    norm_gain = jnp.clip(1.0 + 0.18 * jax.random.normal(seeds[2], (SECTIONS, D), jnp.float32), 0.1, 1.9)
    router_weight = gaussian(seeds[3], (SECTIONS, D, EXPERTS), D ** -0.5, 0.125, ((0, 8),))
    w_gate = gaussian(seeds[4], (SECTIONS, EXPERTS, D, FF), D ** -0.5, 0.125, ((0, 8), (1, 32)))
    w_up = gaussian(seeds[5], (SECTIONS, EXPERTS, D, FF), D ** -0.5, 0.125, ((0, 8), (1, 32)))
    w_down = gaussian(seeds[6], (SECTIONS, EXPERTS, FF, D), FF ** -0.5, 0.21875, ((0, 8), (1, 32)))
    return {"tokens": tokens, "routes": routes, "norm_gain": norm_gain, "router_weight": router_weight, "w_gate": w_gate, "w_up": w_up, "w_down": w_down}


def slot_ranks(route_block):
    flat_routes = route_block.reshape(-1)
    hits = (flat_routes[:, None] == jnp.arange(EXPERTS, dtype=jnp.int32)[None, :]).astype(jnp.int32)
    ranks = lax.optimization_barrier(jnp.sum(jnp.cumsum(hits, axis=0) * hits, axis=1)) - 1
    return ranks.reshape(route_block.shape).astype(jnp.int32)

def expert_ffn(slot_block, gate_matrix, up_matrix, down_matrix):
    gate_part = jnp.dot(slot_block, gate_matrix, preferred_element_type=jnp.float32)
    up_part = jnp.dot(slot_block, up_matrix, preferred_element_type=jnp.float32)
    hidden = (jax.nn.silu(gate_part) * up_part).astype(jnp.bfloat16)
    return jnp.dot(hidden, down_matrix, preferred_element_type=jnp.float32).astype(jnp.bfloat16)

def reference(tokens, routes, norm_gain, router_weight, w_gate, w_up, w_down):
    outputs = []
    token_index = jnp.arange(TOKENS, dtype=jnp.int32)
    source = (token_index // TOK_DEV).astype(jnp.int32)
    for section in range(SECTIONS):
        wide_rows = tokens[section].astype(jnp.float32)
        mean_square = lax.optimization_barrier(jnp.mean(wide_rows * wide_rows, axis=-1, keepdims=True))
        normed = (wide_rows * lax.rsqrt(mean_square + 1e-06) * norm_gain[section]).astype(jnp.bfloat16)
        score = jax.nn.sigmoid(jnp.dot(normed, router_weight[section], preferred_element_type=jnp.float32))
        route_now = routes[section]
        picked = jnp.take_along_axis(score, route_now, axis=1)
        gate_values = (picked / lax.optimization_barrier(jnp.sum(picked, axis=1, keepdims=True))).astype(jnp.bfloat16)
        blocks = route_now.reshape(N_EXPERT, TOK_DEV, TOP)
        ranks = jax.vmap(slot_ranks)(blocks).reshape(TOKENS, TOP)
        positions = (source[:, None] * CAP + ranks).astype(jnp.int32)
        owners = jnp.broadcast_to(token_index[:, None], (TOKENS, TOP)).astype(jnp.int32)
        table = jnp.full((EXPERTS, N_EXPERT * CAP), -1, jnp.int32).at[route_now, positions].set(owners)
        valid = table >= 0
        slot_rows = jnp.where(valid[..., None], normed[jnp.maximum(table, 0)], jnp.zeros((), jnp.bfloat16))
        expert_out = lax.map(lambda pack: expert_ffn(pack[0], pack[1], pack[2], pack[3]), (slot_rows, w_gate[section], w_up[section], w_down[section]))
        picked_out = expert_out[route_now, positions]
        moe = jnp.einsum('tk,tkd->td', gate_values.astype(jnp.float32), picked_out.astype(jnp.float32))
        outputs.append((wide_rows + moe).astype(jnp.bfloat16))
    stacked = jnp.stack(outputs)
    return jnp.roll(stacked, 1, axis=0)
```

```python
import functools

import jax
import jax.numpy as jnp
from jax import lax
from jax.experimental import pallas as pl
from jax.experimental.pallas import tpu as pltpu
from jax.sharding import PartitionSpec as P

MESH = pl.DeviceIdType.MESH
NZ = 8
CAP = 36
GROUP = 4
ROWS = GROUP * CAP
FAR = 1024.0
SLOT = {0: 0, -1: 1, 1: 2, -2: 3, 2: 4, -3: 5, 3: 6, 4: 7, -4: 7}


def kernel(
    nq, tokens, routes, gain, router, wg_hbm, wu_hbm, wd_hbm, out,
    xb, pts, pt, sel, wmap, so, xs, yr, acc_g, acc_u, hid, cb, rss, rsr, outs, wg, wu, wd,
    zs_s, zs_r, pt_s, pt_r, xs_s, xs_r, ys_s, ys_r, rs_s, rs_r, pp_s, pp_r, w_sem,
):
    width = tokens.shape[2]
    tok = tokens.shape[1]
    half = tok // 2
    F = width // nq
    p = lax.axis_index("pipe")
    e = lax.axis_index("expert")
    z, a, c = e // 4, (e // 2) % 2, e % 2
    mine = 2 * a + c

    def at_z(d):
        return {"expert": ((z + d + NZ) % NZ) * 4 + mine}

    level = [mine, 2 * a + (1 - c), 2 * (1 - a) + c, 2 * (1 - a) + (1 - c)]

    def at_level(t):
        return {"expert": z * 4 + level[t]}

    barrier = pltpu.get_barrier_semaphore()
    for d in range(1, NZ):
        pl.semaphore_signal(barrier, inc=1, device_id=at_z(d), device_id_type=MESH)
    for t in (1, 2, 3):
        pl.semaphore_signal(barrier, inc=1, device_id=at_level(t), device_id_type=MESH)
    pl.semaphore_signal(barrier, inc=1, device_id={"pipe": (p + 7) % 8}, device_id_type=MESH)

    w_copies = [
        pltpu.make_async_copy(wg_hbm.at[0, 0], wg, w_sem.at[0]),
        pltpu.make_async_copy(wu_hbm.at[0, 0], wu, w_sem.at[1]),
        pltpu.make_async_copy(wd_hbm.at[0, 0], wd, w_sem.at[2]),
    ]
    for w_copy in w_copies:
        w_copy.start()

    def remote(src, dst, s_sem, r_sem, where):
        return pltpu.make_async_remote_copy(
            src_ref=src, dst_ref=dst, send_sem=s_sem, recv_sem=r_sem, device_id=where, device_id_type=MESH
        )

    def z_copy(q, way, s):
        sign = 1 - 2 * way
        src, dst = xb.at[q, SLOT[-(s - 1) * sign]], xb.at[q, SLOT[-s * sign]]
        if s == 4:
            part = pl.ds(way * half, half)
            src, dst = src.at[part], dst.at[part]
        return remote(src, dst, zs_s.at[q, way, s - 1], zs_r.at[q, way, s - 1], at_z(sign))

    def pt_copy(d):
        return remote(pts.at[(z + d + NZ) % NZ], pt.at[SLOT[-d]], pt_s.at[SLOT[-d]], pt_r.at[SLOT[-d]], at_z(d))

    def x_copy(q, t):
        return remote(so.at[q, level[t]], xs.at[q, mine], xs_s.at[q, t], xs_r.at[q, t], at_level(t))

    def x_own(q):
        return pltpu.make_async_copy(so.at[q, mine], xs.at[q, mine], xs_r.at[q, 0])

    def y_copy(q, t):
        return remote(so.at[q, level[t]], yr.at[q, :, mine], ys_s.at[q, t], ys_r.at[q, t], at_level(t))

    def y_own(q):
        return pltpu.make_async_copy(so.at[q, mine], yr.at[q, :, mine], ys_r.at[q, 0])

    def rs_copy(q, way, s):
        sign = 1 - 2 * way
        src, dst = rss.at[q, way, s], rsr.at[q, way, s]
        if s == 0:
            part = pl.ds(way * half, half)
            src, dst = src.at[part], dst.at[part]
        return remote(src, dst, rs_s.at[q, way, s], rs_r.at[q, way, s], at_z(sign))

    def pipe_copy(q):
        return remote(
            outs.at[q], out.at[0, :, pl.ds(pl.multiple_of(q * F, F), F)], pp_s.at[q], pp_r.at[q], {"pipe": (p + 1) % 8}
        )

    wide = tokens[0].astype(jnp.float32)
    mean_square = jnp.mean(wide * wide, axis=-1, keepdims=True)
    normed = (wide * lax.rsqrt(mean_square + 1e-06) * gain[...]).astype(jnp.bfloat16)
    for q in range(nq):
        xb[q, 0] = normed[:, q * F : (q + 1) * F]

    pl.semaphore_wait(barrier, 11)
    for way in (0, 1):
        z_copy(0, way, 1).start()

    lane = lax.broadcasted_iota(jnp.int32, (1, 16 * NZ), 1)
    kind = lane % 16
    expert_of = 4 * (lane // 16) + lane % 4
    spread = (lax.broadcasted_iota(jnp.int32, (router.shape[2], 16 * NZ), 0) == expert_of).astype(jnp.bfloat16)
    wide_router = jnp.dot(router[0], spread, preferred_element_type=jnp.float32).astype(jnp.bfloat16)
    score = jax.nn.sigmoid(jnp.dot(normed, wide_router, preferred_element_type=jnp.float32))
    hit = jnp.zeros((tok, 16 * NZ), jnp.float32)
    for k in range(routes.shape[2]):
        hit = hit + (routes[0, :, k : k + 1] == expert_of).astype(jnp.float32)
    earlier = (
        lax.broadcasted_iota(jnp.int32, (tok, tok), 1) < lax.broadcasted_iota(jnp.int32, (tok, tok), 0)
    ).astype(jnp.bfloat16)
    rank = jnp.dot(earlier, hit.astype(jnp.bfloat16), preferred_element_type=jnp.float32)
    total = jnp.sum(jnp.where(kind < 4, hit * score, 0.0), axis=1, keepdims=True)
    gate = score / total
    packed = jnp.where(
        kind < 4, jnp.where(hit > 0.0, rank, FAR), jnp.where((kind < 8) & (hit > 0.0), gate, 0.0)
    )
    pts[...] = jnp.transpose(packed).astype(jnp.bfloat16).reshape(NZ, 16, tok)
    for d in range(1, NZ):
        pt_copy(d if d <= 4 else d - NZ).start()
    pt[0] = pts[z]

    def build_sel():
        for d in range(1, NZ):
            pt_copy(d if d <= 4 else d - NZ).wait_recv()
        row = lax.broadcasted_iota(jnp.int32, (ROWS, tok), 0).astype(jnp.float32)
        for g in range(2):
            for i in range(GROUP):
                tile = pt[g * GROUP + i].astype(jnp.float32)
                for j in range(4):
                    same = (row - float(CAP * i)) == tile[j : j + 1, :]
                    sel[g, j * ROWS : (j + 1) * ROWS, i * tok : (i + 1) * tok] = jnp.where(same, 1.0, 0.0).astype(
                        jnp.bfloat16
                    )

    def build_wmap():
        turned = jnp.transpose(pt[...].reshape(16 * NZ, tok).astype(jnp.float32))
        col = lax.broadcasted_iota(jnp.int32, (tok, 4 * ROWS), 1).astype(jnp.float32)
        for g in range(2):
            for i in range(GROUP):
                first = (g * GROUP + i) * 16
                value = jnp.zeros((tok, 4 * ROWS), jnp.float32)
                for j in range(4):
                    place = turned[:, first + j : first + j + 1] + float(ROWS * j + CAP * i)
                    weight = turned[:, first + 4 + j : first + 5 + j]
                    value = jnp.where(col == place, weight, value)
                wmap[g, i * tok : (i + 1) * tok] = value.astype(jnp.bfloat16)

    def valid(q, body):
        @pl.when((q >= 0) & (q < nq))
        def _():
            body(q)

    def forward(s):
        def body(q):
            for way in (0, 1):
                if s > 1:
                    z_copy(q, way, s - 1).wait_recv()
                z_copy(q, way, s).start()

        return body

    def select(q):
        for way in (0, 1):
            z_copy(q, way, 4).wait_recv()
        for g in range(2):
            block = xb[q, g * GROUP : (g + 1) * GROUP].reshape(GROUP * tok, F)
            picked = jnp.dot(sel[g], block, preferred_element_type=jnp.float32).astype(jnp.bfloat16)
            for j in range(4):
                so[q, j, g] = picked[j * ROWS : (j + 1) * ROWS]
        for t in (2, 3, 1):
            x_copy(q, t).start()
        x_own(q).start()

    def accumulate(q):
        for t in (1, 2, 3):
            x_copy(q, t).wait_recv()
        x_own(q).wait()
        rows = xs[q].reshape(8 * ROWS, F)
        part = pl.ds(pl.multiple_of(q * F, F), F)
        acc_g[...] += jnp.dot(rows, wg[part], preferred_element_type=jnp.float32)
        acc_u[...] += jnp.dot(rows, wu[part], preferred_element_type=jnp.float32)

    LAG = 1

    def gather_tick(tau, carry):
        valid(tau - 4, select)
        for s in (4, 3, 2):
            valid(tau - s + 1, forward(s))

        @pl.when(tau > 0)
        def _():
            valid(tau, forward(1))

        valid(tau - 4 - LAG, accumulate)
        return carry

    lax.fori_loop(0, 4, gather_tick, 0)
    build_sel()
    acc_g[...] = jnp.zeros_like(acc_g)
    acc_u[...] = jnp.zeros_like(acc_u)
    for w_copy in w_copies:
        w_copy.wait()
    lax.fori_loop(4, 6, gather_tick, 0)
    build_wmap()
    lax.fori_loop(6, nq + 4 + LAG, gather_tick, 0)

    def act(k, carry):
        part = pl.ds(pl.multiple_of(k * ROWS, ROWS), ROWS)
        v = acc_g[part]
        hid[part] = (v / (1.0 + jnp.exp(-v)) * acc_u[part]).astype(jnp.bfloat16)
        return carry

    lax.fori_loop(0, 8, act, 0)

    def sent(q, carry):
        for t in (1, 2, 3):
            x_copy(q, t).wait_send()
        return carry

    lax.fori_loop(0, nq, sent, 0)

    def produce(q):
        part = pl.ds(pl.multiple_of(q * F, F), F)
        y = jnp.dot(hid[...], wd[:, part], preferred_element_type=jnp.float32).astype(jnp.bfloat16)
        for k in range(4):
            for g in range(2):
                n = (2 * k + g) * ROWS
                so[q, k, g] = y[n : n + ROWS]
        for t in (2, 3, 1):
            y_copy(q, t).start()
        y_own(q).start()

    def unselect(q):
        for t in (1, 2, 3):
            y_copy(q, t).wait_recv()
        y_own(q).wait()
        for g in (1, 0):
            rows = yr[q, g].reshape(4 * ROWS, F)
            sums = jnp.dot(wmap[g], rows, preferred_element_type=jnp.float32)
            for i in range(GROUP):
                block = sums[i * tok : (i + 1) * tok]
                if g * GROUP + i == 7:
                    rss[q, 0, 0] = block.astype(jnp.bfloat16)
                    rss[q, 1, 0] = block.astype(jnp.bfloat16)
                else:
                    cb[q, g * GROUP + i] = block
            if g == 1:
                for way in (0, 1):
                    rs_copy(q, way, 0).start()

    def pass_on(s):
        def body(q):
            for way in (0, 1):
                rs_copy(q, way, s - 1).wait_recv()
                sign = 1 - 2 * way
                slot = SLOT[(4 - s) * sign]
                if s == 1:
                    add, keep = slice(way * half, (way + 1) * half), slice((1 - way) * half, (2 - way) * half)
                    rss[q, way, s, add] = (
                        cb[q, slot, add] + rsr[q, way, s - 1, add].astype(jnp.float32)
                    ).astype(jnp.bfloat16)
                    rss[q, way, s, keep] = cb[q, slot, keep].astype(jnp.bfloat16)
                else:
                    rss[q, way, s] = (cb[q, slot] + rsr[q, way, s - 1].astype(jnp.float32)).astype(jnp.bfloat16)
                rs_copy(q, way, s).start()

        return body

    def finish(q):
        for way in (0, 1):
            rs_copy(q, way, 3).wait_recv()
        part = pl.ds(pl.multiple_of(q * F, F), F)
        moe = cb[q, 0] + rsr[q, 0, 3].astype(jnp.float32) + rsr[q, 1, 3].astype(jnp.float32)
        outs[q] = (tokens[0, :, part].astype(jnp.float32) + moe).astype(jnp.bfloat16)
        pipe_copy(q).start()

    LEAD = 2
    for q in range(LEAD):
        produce(q)

    def combine_tick(tau, carry):
        valid(tau - 4, finish)
        for s in (3, 2, 1):
            valid(tau - s, pass_on(s))
        valid(tau, unselect)

        @pl.when(tau + LEAD < nq)
        def _():
            produce(tau + LEAD)

        return carry

    lax.fori_loop(0, nq + 4, combine_tick, 0)

    def drain(q, carry):
        for way in (0, 1):
            for s in range(1, 5):
                z_copy(q, way, s).wait_send()
            for s in range(4):
                rs_copy(q, way, s).wait_send()
        for t in (1, 2, 3):
            y_copy(q, t).wait_send()
        pipe_copy(q).wait()
        return carry

    for d in range(1, NZ):
        pt_copy(d if d <= 4 else d - NZ).wait_send()
    lax.fori_loop(0, nq, drain, 0)


def local(tokens, routes, norm_gain, router_weight, w_gate, w_up, w_down):
    tok, width = tokens.shape[1:]
    ff = w_gate.shape[3]
    nq = 8
    F = width // nq
    bf, f32 = jnp.bfloat16, jnp.float32
    vmem = pl.BlockSpec(memory_space=pltpu.VMEM)
    anywhere = pl.BlockSpec(memory_space=pl.ANY)
    dma = pltpu.SemaphoreType.DMA
    return pl.pallas_call(
        functools.partial(kernel, nq),
        out_shape=jax.ShapeDtypeStruct(tokens.shape, bf),
        in_specs=[vmem, vmem, vmem, vmem, anywhere, anywhere, anywhere],
        out_specs=anywhere,
        scratch_shapes=[
            pltpu.VMEM((nq, NZ, tok, F), bf),
            pltpu.VMEM((NZ, 16, tok), bf),
            pltpu.VMEM((NZ, 16, tok), bf),
            pltpu.VMEM((2, 4 * ROWS, GROUP * tok), bf),
            pltpu.VMEM((2, GROUP * tok, 4 * ROWS), bf),
            pltpu.VMEM((nq, 4, 2, ROWS, F), bf),
            pltpu.VMEM((nq, 4, 2, ROWS, F), bf),
            pltpu.VMEM((nq, 2, 4, ROWS, F), bf),
            pltpu.VMEM((8 * ROWS, ff), f32),
            pltpu.VMEM((8 * ROWS, ff), f32),
            pltpu.VMEM((8 * ROWS, ff), bf),
            pltpu.VMEM((nq, 7, tok, F), f32),
            pltpu.VMEM((nq, 2, 4, tok, F), bf),
            pltpu.VMEM((nq, 2, 4, tok, F), bf),
            pltpu.VMEM((nq, tok, F), bf),
            pltpu.VMEM((width, ff), bf),
            pltpu.VMEM((width, ff), bf),
            pltpu.VMEM((ff, width), bf),
            dma((nq, 2, 4)),
            dma((nq, 2, 4)),
            dma((NZ,)),
            dma((NZ,)),
            dma((nq, 4)),
            dma((nq, 4)),
            dma((nq, 4)),
            dma((nq, 4)),
            dma((nq, 2, 4)),
            dma((nq, 2, 4)),
            dma((nq,)),
            dma((nq,)),
            dma((3,)),
        ],
        compiler_params=pltpu.CompilerParams(
            collective_id=0, has_side_effects=True, vmem_limit_bytes=62 * 2**20
        ),
        name="relay_moe",
    )(tokens, routes, norm_gain, router_weight, w_gate, w_up, w_down)


def solution(mesh):
    return jax.shard_map(
        local,
        mesh=mesh,
        in_specs=(
            P("pipe", "expert", None),
            P("pipe", "expert", None),
            P("pipe", None),
            P("pipe", None, None),
            P("pipe", "expert", None, None),
            P("pipe", "expert", None, None),
            P("pipe", "expert", None, None),
        ),
        out_specs=P("pipe", "expert", None),
        check_vma=False,
    )
```

```python
import functools

import jax
import jax.numpy as jnp
from jax import lax
from jax.experimental import pallas as pl
from jax.experimental.pallas import tpu as pltpu
from jax.sharding import PartitionSpec as P

MESH = pl.DeviceIdType.MESH
NZ = 8
CAP = 36
GROUP = 4
ROWS = GROUP * CAP
KEPT = 4
FAR = 1024.0
SLOT = {0: 0, -1: 1, 1: 2, -2: 3, 2: 4, -3: 5, 3: 6, 4: 7, -4: 7}


def kernel(
    nq, tokens, routes, gain, router, wg_hbm, wu_hbm, wd_hbm, out,
    xb, xe, pts, pt, sel, wmap, sel_e, wmap_e, so, xs, yr, yr_e, acc_g, acc_u, hid, cb, cb_e, rss, rsr, rss_e, rsr_e,
    last, outs, wg, wu, wd,
    zs_s, zs_r, pt_s, pt_r, xs_s, xs_r, ys_s, ys_r, rs_s, rs_r, ex_s, ex_r, pp_s, pp_r, w_sem,
):
    width = tokens.shape[2]
    tok = tokens.shape[1]
    half = tok // 2
    F = width // nq
    E = nq - 1
    p = lax.axis_index("pipe")
    e = lax.axis_index("expert")
    z, a, c = e // 4, (e // 2) % 2, e % 2
    mine = 2 * a + c

    def at_z(d):
        return {"expert": ((z + d + NZ) % NZ) * 4 + mine}

    def across(d):
        return {"expert": ((z + d + NZ) % NZ) * 4 + 2 * (1 - a) + c}

    level = [mine, 2 * a + (1 - c), 2 * (1 - a) + c, 2 * (1 - a) + (1 - c)]

    def at_level(t):
        return {"expert": z * 4 + level[t]}

    barrier = pltpu.get_barrier_semaphore()
    for d in range(1, NZ):
        pl.semaphore_signal(barrier, inc=1, device_id=at_z(d), device_id_type=MESH)
        pl.semaphore_signal(barrier, inc=1, device_id=across(d), device_id_type=MESH)
    for t in (1, 2, 3):
        pl.semaphore_signal(barrier, inc=1, device_id=at_level(t), device_id_type=MESH)
    pl.semaphore_signal(barrier, inc=1, device_id={"pipe": (p + 7) % 8}, device_id_type=MESH)

    w_copies = [
        pltpu.make_async_copy(wg_hbm.at[0, 0], wg, w_sem.at[0]),
        pltpu.make_async_copy(wu_hbm.at[0, 0], wu, w_sem.at[1]),
        pltpu.make_async_copy(wd_hbm.at[0, 0], wd, w_sem.at[2]),
    ]
    for w_copy in w_copies:
        w_copy.start()

    def remote(src, dst, s_sem, r_sem, where):
        return pltpu.make_async_remote_copy(
            src_ref=src, dst_ref=dst, send_sem=s_sem, recv_sem=r_sem, device_id=where, device_id_type=MESH
        )

    def z_copy(q, way, s):
        sign = 1 - 2 * way
        src, dst = xb.at[q, SLOT[-(s - 1) * sign]], xb.at[q, SLOT[-s * sign]]
        if s == 4:
            part = pl.ds(way * half, half)
            src, dst = src.at[part], dst.at[part]
        return remote(src, dst, zs_s.at[q, way, s - 1], zs_r.at[q, way, s - 1], at_z(sign))

    def ze_copy(way, s):
        sign = 1 - 2 * way
        src, dst = xe.at[:, SLOT[-(s - 1) * sign]], xe.at[:, SLOT[-s * sign]]
        if s == 4:
            part = pl.ds(way * half, half)
            src, dst = src.at[:, part], dst.at[:, part]
        return remote(src, dst, zs_s.at[E, way, s - 1], zs_r.at[E, way, s - 1], at_z(sign))

    def pt_copy(d, col):
        n = SLOT[-d] if d else 0
        return remote(
            pts.at[(z + d + NZ) % NZ], pt.at[col, n], pt_s.at[col, n], pt_r.at[col, n], across(d) if col else at_z(d)
        )

    pt_all = [(d, col) for d in (1, -1, 2, -2, 3, -3, 4, 0) for col in (0, 1) if d or col]

    def x_copy(q, t, g):
        return remote(
            so.at[q, level[t], g], xs.at[q, a, c, g], xs_s.at[q, t, g], xs_r.at[q, t, g], at_level(t)
        )

    def x_own(q, g):
        return pltpu.make_async_copy(so.at[q, mine, g], xs.at[q, a, c, g], xs_r.at[q, 0, g])

    def xe_copy():
        return remote(
            so.at[E, pl.ds(2 * (1 - c), 2)], xs.at[E, :, c], xs_s.at[E, 1, 0], xs_r.at[E, 1, 0], at_level(1)
        )

    def xe_own():
        return pltpu.make_async_copy(so.at[E, pl.ds(2 * c, 2)], xs.at[E, :, c], xs_r.at[E, 0, 0])

    def y_copy(q, t, g):
        return remote(so.at[q, level[t], g], yr.at[q, g, mine], ys_s.at[q, t, g], ys_r.at[q, t, g], at_level(t))

    def y_own(q, g):
        return pltpu.make_async_copy(so.at[q, mine, g], yr.at[q, g, mine], ys_r.at[q, 0, g])

    def ye_copy():
        return remote(
            so.at[E, pl.ds(2 * (1 - c), 2)], yr_e.at[:, :, c], ys_s.at[E, 1, 0], ys_r.at[E, 1, 0], at_level(1)
        )

    def ye_own():
        return pltpu.make_async_copy(so.at[E, pl.ds(2 * c, 2)], yr_e.at[:, :, c], ys_r.at[E, 0, 0])

    def early_copy():
        return remote(xe.at[0, 0], xe.at[1, 0], ex_s.at[0], ex_r.at[0], at_level(2))

    def late_copy():
        return remote(last.at[0], last.at[1], ex_s.at[1], ex_r.at[1], at_level(2))

    def rs_copy(q, way, s):
        sign = 1 - 2 * way
        src, dst = rss.at[q, way, s], rsr.at[q, way, s]
        if s == 0:
            part = pl.ds(way * half, half)
            src, dst = src.at[part], dst.at[part]
        return remote(src, dst, rs_s.at[q, way, s], rs_r.at[q, way, s], at_z(sign))

    def rse_copy(way, s):
        sign = 1 - 2 * way
        src, dst = rss_e.at[way, s], rsr_e.at[way, s]
        if s == 0:
            part = pl.ds(way * half, half)
            src, dst = src.at[:, part], dst.at[:, part]
        return remote(src, dst, rs_s.at[E, way, s], rs_r.at[E, way, s], at_z(sign))

    def pipe_copy(q):
        return remote(
            outs.at[q], out.at[0, :, pl.ds(pl.multiple_of(q * F, F), F)], pp_s.at[q], pp_r.at[q], {"pipe": (p + 1) % 8}
        )

    wide = tokens[0].astype(jnp.float32)
    mean_square = jnp.mean(wide * wide, axis=-1, keepdims=True)
    normed = (wide * lax.rsqrt(mean_square + 1e-06) * gain[...]).astype(jnp.bfloat16)
    for q in range(E):
        xb[q, 0] = normed[:, q * F : (q + 1) * F]
    xe[0, 0] = normed[:, E * F :]

    pl.semaphore_wait(barrier, 18)
    for way in (0, 1):
        z_copy(0, way, 1).start()
    early_copy().start()

    line = lax.broadcasted_iota(jnp.int32, (16 * NZ, 1), 0)
    kind = line % 16
    expert_of = 4 * (line // 16) + line % 4
    spread = (lax.broadcasted_iota(jnp.int32, (16 * NZ, router.shape[1]), 1) == expert_of).astype(jnp.bfloat16)
    tall_router = jnp.dot(spread, router[0], preferred_element_type=jnp.float32).astype(jnp.bfloat16)
    score = jax.nn.sigmoid(
        lax.dot_general(tall_router, normed, (((1,), (1,)), ((), ())), preferred_element_type=jnp.float32)
    )
    hit = jnp.zeros((16 * NZ, tok), jnp.float32)
    for k in range(routes.shape[0]):
        hit = hit + (routes[k] == expert_of).astype(jnp.float32)
    later = (
        lax.broadcasted_iota(jnp.int32, (tok, tok), 0) < lax.broadcasted_iota(jnp.int32, (tok, tok), 1)
    ).astype(jnp.bfloat16)
    rank = jnp.dot(hit.astype(jnp.bfloat16), later, preferred_element_type=jnp.float32)
    total = jnp.sum(jnp.where(kind < 4, hit * score, 0.0), axis=0, keepdims=True)
    gate = score / total
    packed = jnp.where(
        kind < 4, jnp.where(hit > 0.0, rank, FAR), jnp.where((kind < 8) & (hit > 0.0), gate, 0.0)
    )
    pts[...] = packed.astype(jnp.bfloat16).reshape(NZ, 16, tok)
    for d, col in pt_all:
        pt_copy(d, col).start()
    pt[0, 0] = pts[z]

    def of_chip(first, second):
        return jnp.where(a == 0, first, second)

    def build_sel():
        for d, col in pt_all:
            pt_copy(d, col).wait_recv()
        row = lax.broadcasted_iota(jnp.int32, (ROWS, tok), 0).astype(jnp.float32)
        for g in range(2):
            for i in range(GROUP):
                tile = pt[0, g * GROUP + i].astype(jnp.float32)
                for j in range(4):
                    same = (row - float(CAP * i)) == tile[j : j + 1, :]
                    sel[g, j * ROWS : (j + 1) * ROWS, i * tok : (i + 1) * tok] = jnp.where(same, 1.0, 0.0).astype(
                        jnp.bfloat16
                    )

    def build_sel_e():
        row = lax.broadcasted_iota(jnp.int32, (ROWS, tok), 0).astype(jnp.float32)
        for g in range(2):
            for i in range(GROUP):
                tile = pt[1, g * GROUP + i].astype(jnp.float32)
                for j in range(2):
                    same = (row - float(CAP * i)) == of_chip(tile[j : j + 1, :], tile[2 + j : 3 + j, :])
                    sel_e[g, j * ROWS : (j + 1) * ROWS, i * tok : (i + 1) * tok] = jnp.where(same, 1.0, 0.0).astype(
                        jnp.bfloat16
                    )

    def build_wmap(col):
        turned = jnp.transpose(pt[col].reshape(16 * NZ, tok).astype(jnp.float32))
        wide_place = lax.broadcasted_iota(jnp.int32, (tok, 4 * ROWS), 1).astype(jnp.float32)
        place = lax.broadcasted_iota(jnp.int32, (tok, 2 * ROWS), 1).astype(jnp.float32)
        for g in range(2):
            for i in range(GROUP):
                first = (g * GROUP + i) * 16
                rank_of = [turned[:, first + j : first + j + 1] for j in range(4)]
                gate_of = [turned[:, first + 4 + j : first + 5 + j] for j in range(4)]
                part = slice(i * tok, (i + 1) * tok)
                if col == 0:
                    value = jnp.zeros((tok, 4 * ROWS), jnp.float32)
                    for j in range(4):
                        value = jnp.where(wide_place == rank_of[j] + float(ROWS * j + CAP * i), gate_of[j], value)
                    wmap[g, part] = value.astype(jnp.bfloat16)
                value = jnp.zeros((tok, 2 * ROWS), jnp.float32)
                for j in range(2):
                    here = of_chip(rank_of[j], rank_of[2 + j]) + float(ROWS * j + CAP * i)
                    value = jnp.where(place == here, of_chip(gate_of[j], gate_of[2 + j]), value)
                wmap_e[col, g, part] = value.astype(jnp.bfloat16)

    def valid(q, body):
        @pl.when((q >= 0) & (q < E))
        def _():
            body(q)

    def forward(s):
        def body(q):
            for way in (0, 1):
                if s > 1:
                    z_copy(q, way, s - 1).wait_recv()
                z_copy(q, way, s).start()

        return body

    def forward_e(s):
        if s == 1:
            early_copy().wait_recv()
        for way in (0, 1):
            if s > 1:
                ze_copy(way, s - 1).wait_recv()
            ze_copy(way, s).start()

    def select(g):
        def body(q):
            if g == 1:
                for way in (0, 1):
                    z_copy(q, way, 4).wait_recv()
            block = xb[q, g * GROUP : (g + 1) * GROUP].reshape(GROUP * tok, F)
            picked = jnp.dot(sel[g], block, preferred_element_type=jnp.float32).astype(jnp.bfloat16)
            for j in range(4):
                so[q, j, g] = picked[j * ROWS : (j + 1) * ROWS]
            for t in (2, 3, 1):
                x_copy(q, t, g).start()
            x_own(q, g).start()

        return body

    def select_e():
        for way in (0, 1):
            ze_copy(way, 4).wait_recv()
        here = pl.ds(pl.multiple_of(a * 2 * ROWS, 2 * ROWS), 2 * ROWS)
        for g in range(2):
            for col in (0, 1):
                block = xe[col, g * GROUP : (g + 1) * GROUP].reshape(GROUP * tok, F)
                chosen = sel_e[g] if col else sel[g, here]
                picked = jnp.dot(chosen, block, preferred_element_type=jnp.float32).astype(jnp.bfloat16)
                source = 1 - a if col else a
                for j in range(2):
                    so[E, 2 * j + source, g] = picked[j * ROWS : (j + 1) * ROWS]
        xe_copy().start()
        xe_own().start()

    def multiply(q):
        rows = xs[q].reshape(8 * ROWS, F)
        part = pl.ds(pl.multiple_of(q * F, F), F)
        acc_g[...] += jnp.dot(rows, wg[part], preferred_element_type=jnp.float32)
        acc_u[...] += jnp.dot(rows, wu[part], preferred_element_type=jnp.float32)

    def receive(q):
        for g in (0, 1):
            for t in (1, 2, 3):
                x_copy(q, t, g).wait_recv()
            x_own(q, g).wait()

    LAG = 3

    def gather_tick(tau, carry):
        valid(tau - 4, select(1))
        for s in (4, 3, 2, 1):
            if s > 1:
                valid(tau - s + 1, forward(s))
            else:

                @pl.when((tau > 0) & (tau < E))
                def _():
                    forward(1)(tau)

            @pl.when(tau - s + 1 == E)
            def _():
                forward_e(s)

        @pl.when(tau - 4 == E)
        def _():
            select_e()

        valid(tau - 2, select(0))

        def take(q):
            receive(q)
            multiply(q)

        @pl.when(tau < E + 5)
        def _():
            valid(tau - 4 - LAG, take)

        @pl.when(tau == E + 5)
        def _():
            xe_copy().wait_recv()
            xe_own().wait()
            multiply(E)

        @pl.when(tau > E + 5)
        def _():
            valid(tau - 5 - LAG, take)

        return carry

    lax.fori_loop(0, 2, gather_tick, 0)
    build_sel()
    lax.fori_loop(2, 4, gather_tick, 0)
    acc_g[...] = jnp.zeros_like(acc_g)
    acc_u[...] = jnp.zeros_like(acc_u)
    for w_copy in w_copies:
        w_copy.wait()
    build_sel_e()
    lax.fori_loop(4, 6, gather_tick, 0)
    build_wmap(0)
    lax.fori_loop(6, 7, gather_tick, 0)
    build_wmap(1)
    lax.fori_loop(7, nq + 4 + LAG, gather_tick, 0)

    def sent(q, carry):
        for g in (0, 1):
            for t in (1, 2, 3):
                x_copy(q, t, g).wait_send()
        return carry

    lax.fori_loop(0, E, sent, 0)
    xe_copy().wait_send()

    def act(t):
        for h in (0, 1):
            part = pl.ds(pl.multiple_of((2 * level[t] + h) * ROWS, ROWS), ROWS)
            v = acc_g[part]
            hid[part] = (v / (1.0 + jnp.exp(-v)) * acc_u[part]).astype(jnp.bfloat16)

    def produce_for(q, t):
        rows = pl.ds(pl.multiple_of(2 * level[t] * ROWS, 2 * ROWS), 2 * ROWS)
        part = pl.ds(pl.multiple_of(q * F, F), F)
        y = jnp.dot(hid[rows], wd[:, part], preferred_element_type=jnp.float32).astype(jnp.bfloat16)
        for g in (1, 0):
            so[q, level[t], g] = y[g * ROWS : (g + 1) * ROWS]

    def product(q):
        part = pl.ds(pl.multiple_of(q * F, F), F)
        return jnp.dot(hid[...], wd[:, part], preferred_element_type=jnp.float32).astype(jnp.bfloat16)

    def produce(q):
        y = product(q)
        for k in range(4):
            for g in range(2):
                n = (2 * k + g) * ROWS
                so[q, k, g] = y[n : n + ROWS]
        for g in (1, 0):
            for t in (2, 3, 1):
                y_copy(q, t, g).start()
            y_own(q, g).start()

    def produce_e():
        y = product(E)
        for s in range(2):
            for j in range(2):
                for g in range(2):
                    n = ((2 * s + j) * 2 + g) * ROWS
                    so[E, 2 * j + s, g] = y[n : n + ROWS]
        ye_copy().start()
        ye_own().start()

    def unselect(g):
        def body(q):
            for t in (1, 2, 3):
                y_copy(q, t, g).wait_recv()
            y_own(q, g).wait()
            rows = yr[q, g].reshape(4 * ROWS, F)
            sums = jnp.dot(wmap[g], rows, preferred_element_type=jnp.float32)
            for i in range(GROUP):
                block = sums[i * tok : (i + 1) * tok]
                if g * GROUP + i == 7:
                    for way in (0, 1):
                        part = slice(way * half, (way + 1) * half)
                        rss[q, way, 0, part] = block[part].astype(jnp.bfloat16)
                else:
                    cb[q % KEPT, g * GROUP + i] = block
            if g == 1:
                for way in (0, 1):
                    rs_copy(q, way, 0).start()

        return body

    def unselect_e():
        ye_copy().wait_recv()
        ye_own().wait()
        for g in (1, 0):
            for col in (0, 1):
                source = 1 - a if col else a
                rows = yr_e[source, g].reshape(2 * ROWS, F)
                sums = jnp.dot(wmap_e[col, g], rows, preferred_element_type=jnp.float32)
                for i in range(GROUP):
                    block = sums[i * tok : (i + 1) * tok]
                    if g * GROUP + i == 7:
                        for way in (0, 1):
                            part = slice(way * half, (way + 1) * half)
                            rss_e[way, 0, col, part] = block[part].astype(jnp.bfloat16)
                    else:
                        cb_e[col, g * GROUP + i] = block
            if g == 1:
                for way in (0, 1):
                    rse_copy(way, 0).start()

    def step(own, came, sent_on, way, s):
        if s == 1:
            add, keep = slice(way * half, (way + 1) * half), slice((1 - way) * half, (2 - way) * half)
            sent_on[add] = (own[add] + came[add].astype(jnp.float32)).astype(jnp.bfloat16)
            sent_on[keep] = own[keep].astype(jnp.bfloat16)
        else:
            sent_on[...] = (own[...] + came[...].astype(jnp.float32)).astype(jnp.bfloat16)

    def pass_on(s):
        def body(q):
            for way in (0, 1):
                rs_copy(q, way, s - 1).wait_recv()
                slot = SLOT[(4 - s) * (1 - 2 * way)]
                step(cb.at[q % KEPT, slot], rsr.at[q, way, s - 1], rss.at[q, way, s], way, s)
                rs_copy(q, way, s).start()

        return body

    def pass_on_e(s):
        for way in (0, 1):
            rse_copy(way, s - 1).wait_recv()
            slot = SLOT[(4 - s) * (1 - 2 * way)]
            for col in (0, 1):
                step(cb_e.at[col, slot], rsr_e.at[way, s - 1, col], rss_e.at[way, s, col], way, s)
            rse_copy(way, s).start()

    def finish(q):
        for way in (0, 1):
            rs_copy(q, way, 3).wait_recv()
        part = pl.ds(pl.multiple_of(q * F, F), F)
        moe = cb[q % KEPT, 0] + rsr[q, 0, 3].astype(jnp.float32) + rsr[q, 1, 3].astype(jnp.float32)
        outs[q] = (tokens[0, :, part].astype(jnp.float32) + moe).astype(jnp.bfloat16)
        pipe_copy(q).start()

    def cross_e():
        for way in (0, 1):
            rse_copy(way, 3).wait_recv()
        for col in (0, 1):
            total = cb_e[col, 0] + rsr_e[0, 3, col].astype(jnp.float32) + rsr_e[1, 3, col].astype(jnp.float32)
            if col:
                last[0] = total.astype(jnp.bfloat16)
            else:
                cb_e[0, 0] = total
        late_copy().start()

    def finish_e():
        late_copy().wait_recv()
        moe = cb_e[0, 0] + last[1].astype(jnp.float32)
        outs[E] = (tokens[0, :, E * F :].astype(jnp.float32) + moe).astype(jnp.bfloat16)
        pipe_copy(E).start()

    for t in (2, 3, 1, 0):
        act(t)
        produce_for(0, t)
        for g in (1, 0):
            if t:
                y_copy(0, t, g).start()
            else:
                y_own(0, g).start()
    produce_e()
    unselect_e()
    LEAD = 2
    for q in range(1, LEAD):
        produce(q)

    def combine_tick(tau, carry):
        valid(tau - 1, pass_on(2))
        for s in (1, 2, 3):

            @pl.when(tau == s - 1)
            def _():
                pass_on_e(s)

        @pl.when(tau == 3)
        def _():
            cross_e()

        @pl.when(tau == 4)
        def _():
            finish_e()

        valid(tau - 2, finish)
        valid(tau, unselect(1))
        valid(tau - 1, pass_on(3))

        @pl.when(tau + LEAD < E)
        def _():
            produce(tau + LEAD)

        @pl.when(tau < E)
        def _():
            pass_on(1)(tau)
            unselect(0)(tau)

        return carry

    lax.fori_loop(0, E + 2, combine_tick, 0)

    def drain(q, carry):
        for way in (0, 1):
            for s in range(1, 5):
                z_copy(q, way, s).wait_send()
            for s in range(4):
                rs_copy(q, way, s).wait_send()
        for g in (0, 1):
            for t in (1, 2, 3):
                y_copy(q, t, g).wait_send()
        pipe_copy(q).wait()
        return carry

    for d, col in pt_all:
        pt_copy(d, col).wait_send()
    for way in (0, 1):
        for s in range(1, 5):
            ze_copy(way, s).wait_send()
        for s in range(4):
            rse_copy(way, s).wait_send()
    early_copy().wait_send()
    late_copy().wait_send()
    ye_copy().wait_send()
    lax.fori_loop(0, E, drain, 0)
    pipe_copy(E).wait()


def local(tokens, routes, norm_gain, router_weight, w_gate, w_up, w_down):
    tok, width = tokens.shape[1:]
    ff = w_gate.shape[3]
    nq = 8
    F = width // nq
    bf, f32 = jnp.bfloat16, jnp.float32
    vmem = pl.BlockSpec(memory_space=pltpu.VMEM)
    anywhere = pl.BlockSpec(memory_space=pl.ANY)
    dma = pltpu.SemaphoreType.DMA
    return pl.pallas_call(
        functools.partial(kernel, nq),
        out_shape=jax.ShapeDtypeStruct(tokens.shape, bf),
        in_specs=[vmem, vmem, vmem, vmem, anywhere, anywhere, anywhere],
        out_specs=anywhere,
        scratch_shapes=[
            pltpu.VMEM((nq - 1, NZ, tok, F), bf),
            pltpu.VMEM((2, NZ, tok, F), bf),
            pltpu.VMEM((NZ, 16, tok), bf),
            pltpu.VMEM((2, NZ, 16, tok), bf),
            pltpu.VMEM((2, 4 * ROWS, GROUP * tok), bf),
            pltpu.VMEM((2, GROUP * tok, 4 * ROWS), bf),
            pltpu.VMEM((2, 2 * ROWS, GROUP * tok), bf),
            pltpu.VMEM((2, 2, GROUP * tok, 2 * ROWS), bf),
            pltpu.VMEM((nq, 4, 2, ROWS, F), bf),
            pltpu.VMEM((nq, 2, 2, 2, ROWS, F), bf),
            pltpu.VMEM((nq - 1, 2, 4, ROWS, F), bf),
            pltpu.VMEM((2, 2, 2, ROWS, F), bf),
            pltpu.VMEM((8 * ROWS, ff), f32),
            pltpu.VMEM((8 * ROWS, ff), f32),
            pltpu.VMEM((8 * ROWS, ff), bf),
            pltpu.VMEM((KEPT, 7, tok, F), f32),
            pltpu.VMEM((2, 7, tok, F), f32),
            pltpu.VMEM((nq - 1, 2, 4, tok, F), bf),
            pltpu.VMEM((nq - 1, 2, 4, tok, F), bf),
            pltpu.VMEM((2, 4, 2, tok, F), bf),
            pltpu.VMEM((2, 4, 2, tok, F), bf),
            pltpu.VMEM((2, tok, F), bf),
            pltpu.VMEM((nq, tok, F), bf),
            pltpu.VMEM((width, ff), bf),
            pltpu.VMEM((width, ff), bf),
            pltpu.VMEM((ff, width), bf),
            dma((nq, 2, 4)),
            dma((nq, 2, 4)),
            dma((2, NZ)),
            dma((2, NZ)),
            dma((nq, 4, 2)),
            dma((nq, 4, 2)),
            dma((nq, 4, 2)),
            dma((nq, 4, 2)),
            dma((nq, 2, 4)),
            dma((nq, 2, 4)),
            dma((2,)),
            dma((2,)),
            dma((nq,)),
            dma((nq,)),
            dma((3,)),
        ],
        compiler_params=pltpu.CompilerParams(
            collective_id=0, has_side_effects=True, vmem_limit_bytes=62 * 2**20
        ),
        name="relay_moe",
    )(tokens, jnp.transpose(routes, (2, 0, 1)), norm_gain, jnp.swapaxes(router_weight, 1, 2), w_gate, w_up, w_down)


def solution(mesh):
    return jax.shard_map(
        local,
        mesh=mesh,
        in_specs=(
            P("pipe", "expert", None),
            P("pipe", "expert", None),
            P("pipe", None),
            P("pipe", None, None),
            P("pipe", "expert", None, None),
            P("pipe", "expert", None, None),
            P("pipe", "expert", None, None),
        ),
        out_specs=P("pipe", "expert", None),
        check_vma=False,
    )
```

```python
import functools

import jax
import jax.numpy as jnp
from jax import lax
from jax.experimental import pallas as pl
from jax.experimental.pallas import tpu as pltpu
from jax.sharding import PartitionSpec as P

MESH = pl.DeviceIdType.MESH
NZ = 8
CAP = 36
GROUP = 4
ROWS = GROUP * CAP
KEPT = 5
FAR = 1024.0
SLOT = {0: 0, -1: 1, 1: 2, -2: 3, 2: 4, -3: 5, 3: 6, 4: 7, -4: 7}


def kernel(
    nq, tok_hbm, routes, gain, router, wg_hbm, wu_hbm, wd_hbm, out,
    tokens, xb, xe, own_rank, own_gate, pt_rank, pt_gate, sel, wmap, sel_e, wmap_e, so, xs, yr, yr_e, acc_g, acc_u, hid, cb, cb_e, rss, rsr, rss_e, rsr_e,
    last, outs, wg, wu, wd,
    zs_s, zs_r, pt_s, pt_r, xs_s, xs_r, ys_s, ys_r, rs_s, rs_r, ex_s, ex_r, pp_s, pp_r, w_sem,
):
    tok, width = tokens.shape
    tok_copy = pltpu.make_async_copy(tok_hbm.at[0], tokens, w_sem.at[3])
    tok_copy.start()
    half = tok // 2
    F = width // nq
    E = nq - 1
    p = lax.axis_index("pipe")
    e = lax.axis_index("expert")
    z, a, c = e // 4, (e // 2) % 2, e % 2
    mine = 2 * a + c

    def at_z(d):
        return {"expert": ((z + d + NZ) % NZ) * 4 + mine}

    def across(d):
        return {"expert": ((z + d + NZ) % NZ) * 4 + 2 * (1 - a) + c}

    level = [mine, 2 * a + (1 - c), 2 * (1 - a) + c, 2 * (1 - a) + (1 - c)]

    def at_level(t):
        return {"expert": z * 4 + level[t]}

    barrier = pltpu.get_barrier_semaphore()
    for d in range(1, NZ):
        pl.semaphore_signal(barrier, inc=1, device_id=at_z(d), device_id_type=MESH)
        pl.semaphore_signal(barrier, inc=1, device_id=across(d), device_id_type=MESH)
    for t in (1, 2, 3):
        pl.semaphore_signal(barrier, inc=1, device_id=at_level(t), device_id_type=MESH)
    pl.semaphore_signal(barrier, inc=1, device_id={"pipe": (p + 7) % 8}, device_id_type=MESH)

    w_copies = [
        pltpu.make_async_copy(wg_hbm.at[0, 0], wg, w_sem.at[0]),
        pltpu.make_async_copy(wu_hbm.at[0, 0], wu, w_sem.at[1]),
        pltpu.make_async_copy(wd_hbm.at[0, 0], wd, w_sem.at[2]),
    ]
    def remote(src, dst, s_sem, r_sem, where):
        return pltpu.make_async_remote_copy(
            src_ref=src, dst_ref=dst, send_sem=s_sem, recv_sem=r_sem, device_id=where, device_id_type=MESH
        )

    def z_copy(q, way, s):
        sign = 1 - 2 * way
        src, dst = xb.at[q, SLOT[-(s - 1) * sign]], xb.at[q, SLOT[-s * sign]]
        if s == 4:
            part = pl.ds(way * half, half)
            src, dst = src.at[part], dst.at[part]
        return remote(src, dst, zs_s.at[q, way, s - 1], zs_r.at[q, way, s - 1], at_z(sign))

    def ze_copy(way, s):
        sign = 1 - 2 * way
        src, dst = xe.at[:, SLOT[-(s - 1) * sign]], xe.at[:, SLOT[-s * sign]]
        if s == 4:
            part = pl.ds(way * half, half)
            src, dst = src.at[:, part], dst.at[:, part]
        return remote(src, dst, zs_s.at[E, way, s - 1], zs_r.at[E, way, s - 1], at_z(sign))

    def pt_copy(kind, d, col):
        n = SLOT[-d] if d else 0
        mine_all, theirs = ((own_rank, pt_rank), (own_gate, pt_gate))[kind]
        return remote(
            mine_all.at[(z + d + NZ) % NZ],
            theirs.at[col, n],
            pt_s.at[kind, col, n],
            pt_r.at[kind, col, n],
            across(d) if col else at_z(d),
        )

    pt_all = [(d, col) for d in (1, -1, 2, -2, 3, -3, 4, 0) for col in (0, 1) if d or col]

    def x_copy(q, t, g):
        return remote(
            so.at[q, level[t], g], xs.at[q, a, c, g], xs_s.at[q, t, g], xs_r.at[q, t, g], at_level(t)
        )

    def x_own(q, g):
        return pltpu.make_async_copy(so.at[q, mine, g], xs.at[q, a, c, g], xs_r.at[q, 0, g])

    def xe_copy():
        return remote(
            so.at[E, pl.ds(2 * (1 - c), 2)], xs.at[E, :, c], xs_s.at[E, 1, 0], xs_r.at[E, 1, 0], at_level(1)
        )

    def xe_own():
        return pltpu.make_async_copy(so.at[E, pl.ds(2 * c, 2)], xs.at[E, :, c], xs_r.at[E, 0, 0])

    def y_copy(q, t, g):
        return remote(so.at[q, level[t], g], yr.at[q, g, mine], ys_s.at[q, t, g], ys_r.at[q, t, g], at_level(t))

    def y_own(q, g):
        return pltpu.make_async_copy(so.at[q, mine, g], yr.at[q, g, mine], ys_r.at[q, 0, g])

    def ye_copy():
        return remote(
            so.at[E, pl.ds(2 * (1 - c), 2)], yr_e.at[:, :, c], ys_s.at[E, 1, 0], ys_r.at[E, 1, 0], at_level(1)
        )

    def ye_own():
        return pltpu.make_async_copy(so.at[E, pl.ds(2 * c, 2)], yr_e.at[:, :, c], ys_r.at[E, 0, 0])

    def early_copy():
        return remote(xe.at[0, 0], xe.at[1, 0], ex_s.at[0], ex_r.at[0], at_level(2))

    def late_copy():
        return remote(last.at[0], last.at[1], ex_s.at[1], ex_r.at[1], at_level(2))

    def rs_copy(q, way, s):
        sign = 1 - 2 * way
        src, dst = rss.at[q, way, s], rsr.at[q, way, s]
        if s == 0:
            part = pl.ds(way * half, half)
            src, dst = src.at[part], dst.at[part]
        return remote(src, dst, rs_s.at[q, way, s], rs_r.at[q, way, s], at_z(sign))

    def rse_copy(way, s):
        sign = 1 - 2 * way
        src, dst = rss_e.at[way, s], rsr_e.at[way, s]
        if s == 0:
            part = pl.ds(way * half, half)
            src, dst = src.at[:, part], dst.at[:, part]
        return remote(src, dst, rs_s.at[E, way, s], rs_r.at[E, way, s], at_z(sign))

    def pipe_copy(q):
        return remote(
            outs.at[q], out.at[0, :, pl.ds(pl.multiple_of(q * F, F), F)], pp_s.at[q], pp_r.at[q], {"pipe": (p + 1) % 8}
        )

    line = lax.broadcasted_iota(jnp.int32, (16 * NZ, 1), 0)
    expert_of = 4 * (line // 16) + line % 4
    hit = jnp.zeros((16 * NZ, tok), jnp.float32)
    for k in range(routes.shape[0]):
        hit = hit + (routes[k] == expert_of).astype(jnp.float32)
    later = (
        lax.broadcasted_iota(jnp.int32, (tok, tok), 0) < lax.broadcasted_iota(jnp.int32, (tok, tok), 1)
    ).astype(jnp.bfloat16)
    rank = jnp.dot(hit.astype(jnp.bfloat16), later, preferred_element_type=jnp.float32)
    own_rank[...] = jnp.where(hit > 0.0, rank, FAR).astype(jnp.bfloat16).reshape(NZ, 16, tok)
    pt_rank[0, 0] = own_rank[z]

    tok_copy.wait()
    wide = tokens[...].astype(jnp.float32)
    mean_square = jnp.mean(wide * wide, axis=-1, keepdims=True)
    normed = (wide * lax.rsqrt(mean_square + 1e-06) * gain[...]).astype(jnp.bfloat16)
    for q in range(E):
        xb[q, 0] = normed[:, q * F : (q + 1) * F]
    xe[0, 0] = normed[:, E * F :]

    pl.semaphore_wait(barrier, 18)
    for way in (0, 1):
        z_copy(0, way, 1).start()
    for d, col in pt_all:
        pt_copy(0, d, col).start()
    early_copy().start()
    for w_copy in w_copies:
        w_copy.start()

    spread = (lax.broadcasted_iota(jnp.int32, (16 * NZ, router.shape[1]), 1) == expert_of).astype(jnp.bfloat16)
    tall_router = jnp.dot(spread, router[0], preferred_element_type=jnp.float32).astype(jnp.bfloat16)
    score = jax.nn.sigmoid(
        lax.dot_general(tall_router, normed, (((1,), (1,)), ((), ())), preferred_element_type=jnp.float32)
    )
    total = jnp.sum(jnp.where(line % 16 < 4, hit * score, 0.0), axis=0, keepdims=True)
    own_gate[...] = jnp.where(hit > 0.0, score / total, 0.0).astype(jnp.bfloat16).reshape(NZ, 16, tok)
    pt_gate[0, 0] = own_gate[z]

    def of_chip(first, second):
        return jnp.where(a == 0, first, second)

    def build_sel(g):
        for d, col in pt_all:
            if SLOT[-d] // GROUP == g and not col:
                pt_copy(0, d, col).wait_recv()
        row = lax.broadcasted_iota(jnp.int32, (ROWS, tok), 0).astype(jnp.float32)
        for i in range(GROUP):
            tile = pt_rank[0, g * GROUP + i].astype(jnp.float32)
            for j in range(4):
                same = (row - float(CAP * i)) == tile[j : j + 1, :]
                sel[g, j * ROWS : (j + 1) * ROWS, i * tok : (i + 1) * tok] = jnp.where(same, 1.0, 0.0).astype(
                    jnp.bfloat16
                )

    def build_sel_e():
        for d, col in pt_all:
            if col:
                pt_copy(0, d, col).wait_recv()
        row = lax.broadcasted_iota(jnp.int32, (ROWS, tok), 0).astype(jnp.float32)
        for g in range(2):
            for i in range(GROUP):
                tile = pt_rank[1, g * GROUP + i].astype(jnp.float32)
                for j in range(2):
                    same = (row - float(CAP * i)) == of_chip(tile[j : j + 1, :], tile[2 + j : 3 + j, :])
                    sel_e[g, j * ROWS : (j + 1) * ROWS, i * tok : (i + 1) * tok] = jnp.where(same, 1.0, 0.0).astype(
                        jnp.bfloat16
                    )

    def build_wmap(col):
        for d, side in pt_all:
            if side == col:
                pt_copy(1, d, col).wait_recv()
        turned, turned_gate = [
            jnp.transpose(table[col].reshape(16 * NZ, tok).astype(jnp.float32)) for table in (pt_rank, pt_gate)
        ]
        wide_place = lax.broadcasted_iota(jnp.int32, (tok, 4 * ROWS), 1).astype(jnp.float32)
        place = lax.broadcasted_iota(jnp.int32, (tok, 2 * ROWS), 1).astype(jnp.float32)
        for g in range(2):
            for i in range(GROUP):
                first = (g * GROUP + i) * 16
                rank_of = [turned[:, first + j : first + j + 1] for j in range(4)]
                gate_of = [turned_gate[:, first + j : first + j + 1] for j in range(4)]
                part = slice(i * tok, (i + 1) * tok)
                if col == 0:
                    value = jnp.zeros((tok, 4 * ROWS), jnp.float32)
                    for j in range(4):
                        value = jnp.where(wide_place == rank_of[j] + float(ROWS * j + CAP * i), gate_of[j], value)
                    wmap[g, part] = value.astype(jnp.bfloat16)
                value = jnp.zeros((tok, 2 * ROWS), jnp.float32)
                for j in range(2):
                    here = of_chip(rank_of[j], rank_of[2 + j]) + float(ROWS * j + CAP * i)
                    value = jnp.where(place == here, of_chip(gate_of[j], gate_of[2 + j]), value)
                wmap_e[col, g, part] = value.astype(jnp.bfloat16)

    def valid(q, body):
        @pl.when((q >= 0) & (q < E))
        def _():
            body(q)

    def forward(s):
        def body(q):
            for way in (0, 1):
                if s > 1:
                    z_copy(q, way, s - 1).wait_recv()
                z_copy(q, way, s).start()

        return body

    def forward_e(s):
        if s == 1:
            early_copy().wait_recv()
        for way in (0, 1):
            if s > 1:
                ze_copy(way, s - 1).wait_recv()
            ze_copy(way, s).start()

    def select(g):
        def body(q):
            if g == 1:
                for way in (0, 1):
                    z_copy(q, way, 4).wait_recv()
            block = xb[q, g * GROUP : (g + 1) * GROUP].reshape(GROUP * tok, F)
            picked = jnp.dot(sel[g], block, preferred_element_type=jnp.float32).astype(jnp.bfloat16)
            for j in range(4):
                so[q, j, g] = picked[j * ROWS : (j + 1) * ROWS]
            for t in (2, 3, 1):
                x_copy(q, t, g).start()
            x_own(q, g).start()

        return body

    def select_e():
        for way in (0, 1):
            ze_copy(way, 4).wait_recv()
        here = pl.ds(pl.multiple_of(a * 2 * ROWS, 2 * ROWS), 2 * ROWS)
        for g in range(2):
            for col in (0, 1):
                block = xe[col, g * GROUP : (g + 1) * GROUP].reshape(GROUP * tok, F)
                chosen = sel_e[g] if col else sel[g, here]
                picked = jnp.dot(chosen, block, preferred_element_type=jnp.float32).astype(jnp.bfloat16)
                source = 1 - a if col else a
                for j in range(2):
                    so[E, 2 * j + source, g] = picked[j * ROWS : (j + 1) * ROWS]
        xe_copy().start()
        xe_own().start()

    def multiply(q):
        rows = xs[q].reshape(8 * ROWS, F)
        part = pl.ds(pl.multiple_of(q * F, F), F)
        acc_g[...] += jnp.dot(rows, wg[part], preferred_element_type=jnp.float32)
        acc_u[...] += jnp.dot(rows, wu[part], preferred_element_type=jnp.float32)

    def receive(q):
        for g in (0, 1):
            for t in (1, 2, 3):
                x_copy(q, t, g).wait_recv()
            x_own(q, g).wait()

    LAG = 3

    def gather_tick(tau, carry):
        valid(tau - 4, select(1))
        for s in (4, 3, 2, 1):
            if s > 1:
                valid(tau - s + 1, forward(s))
            else:

                @pl.when((tau > 0) & (tau < E))
                def _():
                    forward(1)(tau)

            @pl.when(tau - s + 1 == E)
            def _():
                forward_e(s)

        @pl.when(tau - 4 == E)
        def _():
            select_e()

        valid(tau - 2, select(0))

        def take(q):
            receive(q)
            multiply(q)

        @pl.when(tau < E + 5)
        def _():
            valid(tau - 4 - LAG, take)

        @pl.when(tau == E + 5)
        def _():
            xe_copy().wait_recv()
            xe_own().wait()
            multiply(E)

        @pl.when(tau > E + 5)
        def _():
            valid(tau - 5 - LAG, take)

        return carry

    lax.fori_loop(1, 2, gather_tick, 0)
    build_sel(0)
    lax.fori_loop(2, 3, gather_tick, 0)
    build_sel(1)
    lax.fori_loop(3, 5, gather_tick, 0)
    for d, col in pt_all:
        pt_copy(1, d, col).start()
    acc_g[...] = jnp.zeros_like(acc_g)
    acc_u[...] = jnp.zeros_like(acc_u)
    for w_copy in w_copies:
        w_copy.wait()
    build_sel_e()
    lax.fori_loop(5, 8, gather_tick, 0)
    build_wmap(0)
    lax.fori_loop(8, 9, gather_tick, 0)
    build_wmap(1)
    lax.fori_loop(9, nq + 4 + LAG, gather_tick, 0)

    def sent(q, carry):
        for g in (0, 1):
            for t in (1, 2, 3):
                x_copy(q, t, g).wait_send()
        return carry

    lax.fori_loop(0, E, sent, 0)
    xe_copy().wait_send()

    def act(t):
        for h in (0, 1):
            part = pl.ds(pl.multiple_of((2 * level[t] + h) * ROWS, ROWS), ROWS)
            v = acc_g[part]
            hid[part] = (v / (1.0 + jnp.exp(-v)) * acc_u[part]).astype(jnp.bfloat16)

    def produce_for(q, t):
        rows = pl.ds(pl.multiple_of(2 * level[t] * ROWS, 2 * ROWS), 2 * ROWS)
        part = pl.ds(pl.multiple_of(q * F, F), F)
        y = jnp.dot(hid[rows], wd[:, part], preferred_element_type=jnp.float32).astype(jnp.bfloat16)
        for g in (1, 0):
            so[q, level[t], g] = y[g * ROWS : (g + 1) * ROWS]

    def product(q):
        part = pl.ds(pl.multiple_of(q * F, F), F)
        return jnp.dot(hid[...], wd[:, part], preferred_element_type=jnp.float32).astype(jnp.bfloat16)

    def produce(q):
        y = product(q)
        for k in range(4):
            for g in range(2):
                n = (2 * k + g) * ROWS
                so[q, k, g] = y[n : n + ROWS]
        for g in (1, 0):
            for t in (2, 3, 1):
                y_copy(q, t, g).start()
            y_own(q, g).start()

    def produce_e():
        y = product(E)
        for s in range(2):
            for j in range(2):
                for g in range(2):
                    n = ((2 * s + j) * 2 + g) * ROWS
                    so[E, 2 * j + s, g] = y[n : n + ROWS]
        ye_copy().start()
        ye_own().start()

    def unselect(g):
        def body(q):
            for t in (1, 2, 3):
                y_copy(q, t, g).wait_recv()
            y_own(q, g).wait()
            rows = yr[q, g].reshape(4 * ROWS, F)
            sums = jnp.dot(wmap[g], rows, preferred_element_type=jnp.float32)
            for i in range(GROUP):
                block = sums[i * tok : (i + 1) * tok]
                if g * GROUP + i == 7:
                    for way in (0, 1):
                        part = slice(way * half, (way + 1) * half)
                        rss[q, way, 0, part] = block[part].astype(jnp.bfloat16)
                else:
                    cb[q % KEPT, g * GROUP + i] = block
            if g == 1:
                for way in (0, 1):
                    rs_copy(q, way, 0).start()

        return body

    def unselect_e():
        ye_copy().wait_recv()
        ye_own().wait()
        for g in (1, 0):
            for col in (0, 1):
                source = 1 - a if col else a
                rows = yr_e[source, g].reshape(2 * ROWS, F)
                sums = jnp.dot(wmap_e[col, g], rows, preferred_element_type=jnp.float32)
                for i in range(GROUP):
                    block = sums[i * tok : (i + 1) * tok]
                    if g * GROUP + i == 7:
                        for way in (0, 1):
                            part = slice(way * half, (way + 1) * half)
                            rss_e[way, 0, col, part] = block[part].astype(jnp.bfloat16)
                    else:
                        cb_e[col, g * GROUP + i] = block
            if g == 1:
                for way in (0, 1):
                    rse_copy(way, 0).start()

    def step(own, came, sent_on, way, s):
        if s == 1:
            add, keep = slice(way * half, (way + 1) * half), slice((1 - way) * half, (2 - way) * half)
            sent_on[add] = (own[add] + came[add].astype(jnp.float32)).astype(jnp.bfloat16)
            sent_on[keep] = own[keep].astype(jnp.bfloat16)
        else:
            sent_on[...] = (own[...] + came[...].astype(jnp.float32)).astype(jnp.bfloat16)

    def pass_on(s):
        def body(q):
            for way in (0, 1):
                rs_copy(q, way, s - 1).wait_recv()
                slot = SLOT[(4 - s) * (1 - 2 * way)]
                step(cb.at[q % KEPT, slot], rsr.at[q, way, s - 1], rss.at[q, way, s], way, s)
                rs_copy(q, way, s).start()

        return body

    def pass_on_e(s):
        for way in (0, 1):
            rse_copy(way, s - 1).wait_recv()
            slot = SLOT[(4 - s) * (1 - 2 * way)]
            for col in (0, 1):
                step(cb_e.at[col, slot], rsr_e.at[way, s - 1, col], rss_e.at[way, s, col], way, s)
            rse_copy(way, s).start()

    def finish(q):
        for way in (0, 1):
            rs_copy(q, way, 3).wait_recv()
        part = pl.ds(pl.multiple_of(q * F, F), F)
        moe = cb[q % KEPT, 0] + rsr[q, 0, 3].astype(jnp.float32) + rsr[q, 1, 3].astype(jnp.float32)
        outs[q] = (tokens[:, part].astype(jnp.float32) + moe).astype(jnp.bfloat16)
        pipe_copy(q).start()

    def cross_e():
        for way in (0, 1):
            rse_copy(way, 3).wait_recv()
        for col in (0, 1):
            total = cb_e[col, 0] + rsr_e[0, 3, col].astype(jnp.float32) + rsr_e[1, 3, col].astype(jnp.float32)
            if col:
                last[0] = total.astype(jnp.bfloat16)
            else:
                cb_e[0, 0] = total
        late_copy().start()

    def finish_e():
        late_copy().wait_recv()
        moe = cb_e[0, 0] + last[1].astype(jnp.float32)
        outs[E] = (tokens[:, E * F :].astype(jnp.float32) + moe).astype(jnp.bfloat16)
        pipe_copy(E).start()

    for t in (2, 3, 1, 0):
        act(t)
        produce_for(0, t)
        for g in (1, 0):
            if t:
                y_copy(0, t, g).start()
            else:
                y_own(0, g).start()
    produce_e()
    unselect_e()
    LEAD = 3
    for q in range(1, LEAD):
        produce(q)

    def span(tau, s, body):
        def one(q, carry):
            body(q)
            return carry

        high = jnp.where(tau == E - 2 + s, E, jnp.minimum(tau - s + 1, E - 1))
        lax.fori_loop(jnp.maximum(tau - s, 0), high, one, 0)

    def combine_tick(tau, carry):
        span(tau, 4, finish)
        span(tau, 3, pass_on(3))
        span(tau, 2, pass_on(2))

        @pl.when((tau >= 1) & (tau < E))
        def _():
            pass_on(1)(tau - 1)

        for s in (1, 2, 3):

            @pl.when(tau == s - 1)
            def _():
                pass_on_e(s)

        @pl.when(tau == 3)
        def _():
            cross_e()

        @pl.when(tau == 5)
        def _():
            finish_e()

        valid(tau, unselect(1))

        @pl.when(tau + LEAD < E)
        def _():
            produce(tau + LEAD)

        valid(tau, unselect(0))

        @pl.when(tau == E - 1)
        def _():
            pass_on(1)(tau)

        return carry

    lax.fori_loop(0, E + 3, combine_tick, 0)

    def drain(q, carry):
        for way in (0, 1):
            for s in range(1, 5):
                z_copy(q, way, s).wait_send()
            for s in range(4):
                rs_copy(q, way, s).wait_send()
        for g in (0, 1):
            for t in (1, 2, 3):
                y_copy(q, t, g).wait_send()
        pipe_copy(q).wait()
        return carry

    for d, col in pt_all:
        for kind in (0, 1):
            pt_copy(kind, d, col).wait_send()
    for way in (0, 1):
        for s in range(1, 5):
            ze_copy(way, s).wait_send()
        for s in range(4):
            rse_copy(way, s).wait_send()
    early_copy().wait_send()
    late_copy().wait_send()
    ye_copy().wait_send()
    lax.fori_loop(0, E, drain, 0)
    pipe_copy(E).wait()


def local(tokens, routes, norm_gain, router_weight, w_gate, w_up, w_down):
    tok, width = tokens.shape[1:]
    ff = w_gate.shape[3]
    nq = 8
    F = width // nq
    bf, f32 = jnp.bfloat16, jnp.float32
    vmem = pl.BlockSpec(memory_space=pltpu.VMEM)
    anywhere = pl.BlockSpec(memory_space=pl.ANY)
    dma = pltpu.SemaphoreType.DMA
    return pl.pallas_call(
        functools.partial(kernel, nq),
        out_shape=jax.ShapeDtypeStruct(tokens.shape, bf),
        in_specs=[anywhere, vmem, vmem, vmem, anywhere, anywhere, anywhere],
        out_specs=anywhere,
        scratch_shapes=[
            pltpu.VMEM((tok, width), bf),
            pltpu.VMEM((nq - 1, NZ, tok, F), bf),
            pltpu.VMEM((2, NZ, tok, F), bf),
            pltpu.VMEM((NZ, 16, tok), bf),
            pltpu.VMEM((NZ, 16, tok), bf),
            pltpu.VMEM((2, NZ, 16, tok), bf),
            pltpu.VMEM((2, NZ, 16, tok), bf),
            pltpu.VMEM((2, 4 * ROWS, GROUP * tok), bf),
            pltpu.VMEM((2, GROUP * tok, 4 * ROWS), bf),
            pltpu.VMEM((2, 2 * ROWS, GROUP * tok), bf),
            pltpu.VMEM((2, 2, GROUP * tok, 2 * ROWS), bf),
            pltpu.VMEM((nq, 4, 2, ROWS, F), bf),
            pltpu.VMEM((nq, 2, 2, 2, ROWS, F), bf),
            pltpu.VMEM((nq - 1, 2, 4, ROWS, F), bf),
            pltpu.VMEM((2, 2, 2, ROWS, F), bf),
            pltpu.VMEM((8 * ROWS, ff), f32),
            pltpu.VMEM((8 * ROWS, ff), f32),
            pltpu.VMEM((8 * ROWS, ff), bf),
            pltpu.VMEM((KEPT, 7, tok, F), f32),
            pltpu.VMEM((2, 7, tok, F), f32),
            pltpu.VMEM((nq - 1, 2, 4, tok, F), bf),
            pltpu.VMEM((nq - 1, 2, 4, tok, F), bf),
            pltpu.VMEM((2, 4, 2, tok, F), bf),
            pltpu.VMEM((2, 4, 2, tok, F), bf),
            pltpu.VMEM((2, tok, F), bf),
            pltpu.VMEM((nq, tok, F), bf),
            pltpu.VMEM((width, ff), bf),
            pltpu.VMEM((width, ff), bf),
            pltpu.VMEM((ff, width), bf),
            dma((nq, 2, 4)),
            dma((nq, 2, 4)),
            dma((2, 2, NZ)),
            dma((2, 2, NZ)),
            dma((nq, 4, 2)),
            dma((nq, 4, 2)),
            dma((nq, 4, 2)),
            dma((nq, 4, 2)),
            dma((nq, 2, 4)),
            dma((nq, 2, 4)),
            dma((2,)),
            dma((2,)),
            dma((nq,)),
            dma((nq,)),
            dma((4,)),
        ],
        compiler_params=pltpu.CompilerParams(
            collective_id=0, has_side_effects=True, vmem_limit_bytes=62 * 2**20
        ),
        name="relay_moe",
    )(tokens, jnp.transpose(routes, (2, 0, 1)), norm_gain, jnp.swapaxes(router_weight, 1, 2), w_gate, w_up, w_down)


def solution(mesh):
    return jax.shard_map(
        local,
        mesh=mesh,
        in_specs=(
            P("pipe", "expert", None),
            P("pipe", "expert", None),
            P("pipe", None),
            P("pipe", None, None),
            P("pipe", "expert", None, None),
            P("pipe", "expert", None, None),
            P("pipe", "expert", None, None),
        ),
        out_specs=P("pipe", "expert", None),
        check_vma=False,
    )
```

```python
import functools

import jax
import jax.numpy as jnp
from jax import lax
from jax.experimental import pallas as pl
from jax.experimental.pallas import tpu as pltpu
from jax.sharding import PartitionSpec as P

MESH = pl.DeviceIdType.MESH
NZ = 8
CAP = 36
GROUP = 4
ROWS = GROUP * CAP
NE = 1
KEPT = 4
FAR = 1024.0
SLOT = {0: 0, -1: 1, 1: 2, -2: 3, 2: 4, -3: 5, 3: 6, 4: 7, -4: 7}


def kernel(
    nq, tok_hbm, routes, gain, router, wg_hbm, wu_hbm, wd_hbm, out,
    tokens, xb, xe, own_rank, own_gate, pt_rank, pt_gate, sel, wmap, sel_e, wmap_e, so, xs, yr, yr_e, acc_g, acc_u, hid, cb, cb_e, rsr, rsr_e,
    last, outs, wg, wu, wd,
    zs_s, zs_r, pt_s, pt_r, xs_s, xs_r, ys_s, ys_r, rs_s, rs_r, ex_s, ex_r, pp_s, pp_r, w_sem,
):
    tok, width = tokens.shape
    tok_copy = pltpu.make_async_copy(tok_hbm.at[0], tokens, w_sem.at[3])
    tok_copy.start()
    half = tok // 2
    F = width // nq
    E = nq - NE
    p = lax.axis_index("pipe")
    e = lax.axis_index("expert")
    z, a, c = e // 4, (e // 2) % 2, e % 2
    mine = 2 * a + c

    def at_z(d):
        return {"expert": ((z + d + NZ) % NZ) * 4 + mine}

    level = [mine, 2 * a + (1 - c), 2 * (1 - a) + c, 2 * (1 - a) + (1 - c)]

    def at_level(t):
        return {"expert": z * 4 + level[t]}

    barrier = pltpu.get_barrier_semaphore()
    for d in range(1, NZ):
        pl.semaphore_signal(barrier, inc=1, device_id=at_z(d), device_id_type=MESH)
    for t in (1, 2, 3):
        pl.semaphore_signal(barrier, inc=1, device_id=at_level(t), device_id_type=MESH)
    pl.semaphore_signal(barrier, inc=1, device_id={"pipe": (p + 7) % 8}, device_id_type=MESH)

    w_copies = [
        pltpu.make_async_copy(wg_hbm.at[0, 0], wg, w_sem.at[0]),
        pltpu.make_async_copy(wu_hbm.at[0, 0], wu, w_sem.at[1]),
        pltpu.make_async_copy(wd_hbm.at[0, 0], wd, w_sem.at[2]),
    ]
    def remote(src, dst, s_sem, r_sem, where):
        return pltpu.make_async_remote_copy(
            src_ref=src, dst_ref=dst, send_sem=s_sem, recv_sem=r_sem, device_id=where, device_id_type=MESH
        )

    def z_copy(q, way, s):
        sign = 1 - 2 * way
        src, dst = xb.at[q, SLOT[-(s - 1) * sign]], xb.at[q, SLOT[-s * sign]]
        if s == 4:
            part = pl.ds(way * half, half)
            src, dst = src.at[part], dst.at[part]
        return remote(src, dst, zs_s.at[q, way, s - 1], zs_r.at[q, way, s - 1], at_z(sign))

    def ze_copy(i, way, s):
        sign = 1 - 2 * way
        src, dst = xe.at[i, :, SLOT[-(s - 1) * sign]], xe.at[i, :, SLOT[-s * sign]]
        if s == 4:
            part = pl.ds(way * half, half)
            src, dst = src.at[:, part], dst.at[:, part]
        return remote(src, dst, zs_s.at[E + i, way, s - 1], zs_r.at[E + i, way, s - 1], at_z(sign))

    def pt_copy(kind, d):
        n = SLOT[-d]
        mine_all, theirs = ((own_rank, pt_rank), (own_gate, pt_gate))[kind]
        return remote(
            mine_all.at[(z + d + NZ) % NZ], theirs.at[0, n], pt_s.at[kind, 0, n], pt_r.at[kind, 0, n], at_z(d)
        )

    def pt_share(kind):
        table = (pt_rank, pt_gate)[kind]
        return remote(table.at[0], table.at[1], pt_s.at[kind, 1, 0], pt_r.at[kind, 1, 0], at_level(2))

    pt_all = (1, -1, 2, -2, 3, -3, 4)

    def x_copy(q, t, g):
        return remote(
            so.at[q, level[t], g], xs.at[q, a, c, g], xs_s.at[q, t, g], xs_r.at[q, t, g], at_level(t)
        )

    def x_own(q, g):
        return pltpu.make_async_copy(so.at[q, mine, g], xs.at[q, a, c, g], xs_r.at[q, 0, g])

    def xe_copy(i):
        part = so.at[E + i, pl.ds(2 * (1 - c), 2)]
        return remote(part, xs.at[E + i, :, c], xs_s.at[E + i, 1, 0], xs_r.at[E + i, 1, 0], at_level(1))

    def xe_own(i):
        return pltpu.make_async_copy(so.at[E + i, pl.ds(2 * c, 2)], xs.at[E + i, :, c], xs_r.at[E + i, 0, 0])

    def y_copy(q, t, g):
        return remote(so.at[q, level[t], g], yr.at[q, g, mine], ys_s.at[q, t, g], ys_r.at[q, t, g], at_level(t))

    def y_own(q, g):
        return pltpu.make_async_copy(so.at[q, mine, g], yr.at[q, g, mine], ys_r.at[q, 0, g])

    def ye_copy(i):
        part = so.at[E + i, pl.ds(2 * (1 - c), 2)]
        return remote(part, yr_e.at[i, :, :, c], ys_s.at[E + i, 1, 0], ys_r.at[E + i, 1, 0], at_level(1))

    def ye_own(i):
        return pltpu.make_async_copy(so.at[E + i, pl.ds(2 * c, 2)], yr_e.at[i, :, :, c], ys_r.at[E + i, 0, 0])

    def early_copy(i):
        return remote(xe.at[i, 0, 0], xe.at[i, 1, 0], ex_s.at[i, 0], ex_r.at[i, 0], at_level(2))

    def late_copy(i):
        return remote(last.at[i, 0], last.at[i, 1], ex_s.at[i, 1], ex_r.at[i, 1], at_level(2))

    def rs_copy(q, way, s):
        sign = 1 - 2 * way
        src, dst = xb.at[q, way * 4 + s], rsr.at[q, way, s]
        if s == 0:
            part = pl.ds(way * half, half)
            src, dst = src.at[part], dst.at[part]
        return remote(src, dst, rs_s.at[q, way, s], rs_r.at[q, way, s], at_z(sign))

    def rse_copy(i, way, s):
        sign = 1 - 2 * way
        src, dst = xe.at[i, :, way * 4 + s], rsr_e.at[i, way, s]
        if s == 0:
            part = pl.ds(way * half, half)
            src, dst = src.at[:, part], dst.at[:, part]
        return remote(src, dst, rs_s.at[E + i, way, s], rs_r.at[E + i, way, s], at_z(sign))

    def pipe_copy(q):
        return remote(
            outs.at[q], out.at[0, :, pl.ds(pl.multiple_of(q * F, F), F)], pp_s.at[q], pp_r.at[q], {"pipe": (p + 1) % 8}
        )

    line = lax.broadcasted_iota(jnp.int32, (16 * NZ, 1), 0)
    expert_of = 4 * (line // 16) + line % 4
    hit = jnp.zeros((16 * NZ, tok), jnp.float32)
    for k in range(routes.shape[0]):
        hit = hit + (routes[k] == expert_of).astype(jnp.float32)
    later = (
        lax.broadcasted_iota(jnp.int32, (tok, tok), 0) < lax.broadcasted_iota(jnp.int32, (tok, tok), 1)
    ).astype(jnp.bfloat16)
    rank = jnp.dot(hit.astype(jnp.bfloat16), later, preferred_element_type=jnp.float32)
    own_rank[...] = jnp.where(hit > 0.0, rank, FAR).astype(jnp.bfloat16).reshape(NZ, 16, tok)
    pt_rank[0, 0] = own_rank[z]

    tok_copy.wait()
    wide = tokens[...].astype(jnp.float32)
    mean_square = jnp.mean(wide * wide, axis=-1, keepdims=True)
    normed = (wide * lax.rsqrt(mean_square + 1e-06) * gain[...]).astype(jnp.bfloat16)
    for q in range(E):
        xb[q, 0] = normed[:, q * F : (q + 1) * F]
    for i in range(NE):
        xe[i, 0, 0] = normed[:, (E + i) * F : (E + i + 1) * F]

    pl.semaphore_wait(barrier, 11)
    for way in (0, 1):
        z_copy(0, way, 1).start()
    for d in pt_all:
        pt_copy(0, d).start()
    for i in range(NE):
        early_copy(i).start()
    for w_copy in w_copies:
        w_copy.start()

    spread = (lax.broadcasted_iota(jnp.int32, (16 * NZ, router.shape[1]), 1) == expert_of).astype(jnp.bfloat16)
    tall_router = jnp.dot(spread, router[0], preferred_element_type=jnp.float32).astype(jnp.bfloat16)
    score = jax.nn.sigmoid(
        lax.dot_general(tall_router, normed, (((1,), (1,)), ((), ())), preferred_element_type=jnp.float32)
    )
    total = jnp.sum(jnp.where(line % 16 < 4, hit * score, 0.0), axis=0, keepdims=True)
    own_gate[...] = jnp.where(hit > 0.0, score / total, 0.0).astype(jnp.bfloat16).reshape(NZ, 16, tok)
    pt_gate[0, 0] = own_gate[z]

    def of_chip(first, second):
        return jnp.where(a == 0, first, second)

    def build_sel(g):
        for d in pt_all:
            if SLOT[-d] // GROUP == g:
                pt_copy(0, d).wait_recv()
        row = lax.broadcasted_iota(jnp.int32, (ROWS, tok), 0).astype(jnp.float32)
        for i in range(GROUP):
            tile = pt_rank[0, g * GROUP + i].astype(jnp.float32)
            for j in range(4):
                same = (row - float(CAP * i)) == tile[j : j + 1, :]
                sel[g, j * ROWS : (j + 1) * ROWS, i * tok : (i + 1) * tok] = jnp.where(same, 1.0, 0.0).astype(
                    jnp.bfloat16
                )

    def build_sel_e():
        pt_share(0).wait_recv()
        row = lax.broadcasted_iota(jnp.int32, (ROWS, tok), 0).astype(jnp.float32)
        for g in range(2):
            for i in range(GROUP):
                tile = pt_rank[1, g * GROUP + i].astype(jnp.float32)
                for j in range(2):
                    same = (row - float(CAP * i)) == of_chip(tile[j : j + 1, :], tile[2 + j : 3 + j, :])
                    sel_e[g, j * ROWS : (j + 1) * ROWS, i * tok : (i + 1) * tok] = jnp.where(same, 1.0, 0.0).astype(
                        jnp.bfloat16
                    )

    def build_wmap(col):
        if col == 0:
            for d in pt_all:
                pt_copy(1, d).wait_recv()
            pt_share(1).start()
        else:
            pt_share(1).wait_recv()
        turned, turned_gate = [
            jnp.transpose(table[col].reshape(16 * NZ, tok).astype(jnp.float32)) for table in (pt_rank, pt_gate)
        ]
        wide_place = lax.broadcasted_iota(jnp.int32, (tok, 4 * ROWS), 1).astype(jnp.float32)
        place = lax.broadcasted_iota(jnp.int32, (tok, 2 * ROWS), 1).astype(jnp.float32)
        for g in range(2):
            for i in range(GROUP):
                first = (g * GROUP + i) * 16
                rank_of = [turned[:, first + j : first + j + 1] for j in range(4)]
                gate_of = [turned_gate[:, first + j : first + j + 1] for j in range(4)]
                part = slice(i * tok, (i + 1) * tok)
                if col == 0:
                    value = jnp.zeros((tok, 4 * ROWS), jnp.float32)
                    for j in range(4):
                        value = jnp.where(wide_place == rank_of[j] + float(ROWS * j + CAP * i), gate_of[j], value)
                    wmap[g, part] = value.astype(jnp.bfloat16)
                value = jnp.zeros((tok, 2 * ROWS), jnp.float32)
                for j in range(2):
                    here = of_chip(rank_of[j], rank_of[2 + j]) + float(ROWS * j + CAP * i)
                    value = jnp.where(place == here, of_chip(gate_of[j], gate_of[2 + j]), value)
                wmap_e[col, g, part] = value.astype(jnp.bfloat16)

    def valid(q, body):
        @pl.when((q >= 0) & (q < E))
        def _():
            body(q)

    def forward(s):
        def body(q):
            for way in (0, 1):
                if s > 1:
                    z_copy(q, way, s - 1).wait_recv()
                z_copy(q, way, s).start()

        return body

    def forward_e(i, s):
        if s == 1:
            early_copy(i).wait_recv()
        for way in (0, 1):
            if s > 1:
                ze_copy(i, way, s - 1).wait_recv()
            ze_copy(i, way, s).start()

    def select(g):
        def body(q):
            if g == 1:
                for way in (0, 1):
                    z_copy(q, way, 4).wait_recv()
            block = xb[q, g * GROUP : (g + 1) * GROUP].reshape(GROUP * tok, F)
            picked = jnp.dot(sel[g], block, preferred_element_type=jnp.float32).astype(jnp.bfloat16)
            for j in range(4):
                so[q, j, g] = picked[j * ROWS : (j + 1) * ROWS]
            for t in (2, 3, 1):
                x_copy(q, t, g).start()
            x_own(q, g).start()

        return body

    def select_e(i):
        for way in (0, 1):
            ze_copy(i, way, 4).wait_recv()
        here = pl.ds(pl.multiple_of(a * 2 * ROWS, 2 * ROWS), 2 * ROWS)
        for g in range(2):
            for col in (0, 1):
                block = xe[i, col, g * GROUP : (g + 1) * GROUP].reshape(GROUP * tok, F)
                chosen = sel_e[g] if col else sel[g, here]
                picked = jnp.dot(chosen, block, preferred_element_type=jnp.float32).astype(jnp.bfloat16)
                source = 1 - a if col else a
                for j in range(2):
                    so[E + i, 2 * j + source, g] = picked[j * ROWS : (j + 1) * ROWS]
        xe_copy(i).start()
        xe_own(i).start()

    def multiply(q):
        rows = xs[q].reshape(8 * ROWS, F)
        part = pl.ds(pl.multiple_of(q * F, F), F)
        acc_g[...] += jnp.dot(rows, wg[part], preferred_element_type=jnp.float32)
        acc_u[...] += jnp.dot(rows, wu[part], preferred_element_type=jnp.float32)

    def receive(q):
        for g in (0, 1):
            for t in (1, 2, 3):
                x_copy(q, t, g).wait_recv()
            x_own(q, g).wait()

    LAG = 3

    def gather_tick(tau, carry):
        for s in (4, 3, 2, 1):
            if s > 1:
                valid(tau - s + 1, forward(s))
            else:

                @pl.when((tau > 0) & (tau < E))
                def _():
                    forward(1)(tau)

            @pl.when((tau - s + 1 >= E) & (tau - s + 1 < nq))
            def _():
                forward_e(tau - s + 1 - E, s)

            if s == 3:
                valid(tau - 2, select(0))

        valid(tau - 4, select(1))

        @pl.when((tau - 4 >= E) & (tau - 4 < nq))
        def _():
            select_e(tau - 4 - E)


        def take(q):
            receive(q)
            multiply(q)

        @pl.when((tau - 4 - LAG >= 0) & (tau - 4 - LAG < E - 1))
        def _():
            take(tau - 4 - LAG)

        @pl.when((tau - 5 >= E) & (tau - 5 < nq))
        def _():
            xe_copy(tau - 5 - E).wait_recv()
            xe_own(tau - 5 - E).wait()
            multiply(tau - 5)

        return carry

    lax.fori_loop(1, 2, gather_tick, 0)
    build_sel(0)
    lax.fori_loop(2, 3, gather_tick, 0)
    build_sel(1)
    pt_share(0).start()
    lax.fori_loop(3, 5, gather_tick, 0)
    for d in pt_all:
        pt_copy(1, d).start()
    acc_g[...] = jnp.zeros_like(acc_g)
    acc_u[...] = jnp.zeros_like(acc_u)
    for w_copy in w_copies:
        w_copy.wait()
    lax.fori_loop(5, 7, gather_tick, 0)
    build_sel_e()
    lax.fori_loop(7, 8, gather_tick, 0)
    build_wmap(0)
    lax.fori_loop(8, 9, gather_tick, 0)
    build_wmap(1)
    lax.fori_loop(9, max(nq + 5, E + 3 + LAG), gather_tick, 0)

    def sent(q, carry):
        for way in (0, 1):
            for s in range(1, 5):
                z_copy(q, way, s).wait_send()
        for g in (0, 1):
            for t in (1, 2, 3):
                x_copy(q, t, g).wait_send()
        return carry

    sides = [(a, c), (a, 1 - c), (1 - a, c), (1 - a, 1 - c)]

    def act(t):
        part = pl.ds(pl.multiple_of(2 * level[t] * ROWS, 2 * ROWS), 2 * ROWS)
        rows = xs[(E - 1, *sides[t])].reshape(2 * ROWS, F)
        slab = slice((E - 1) * F, E * F)
        v = acc_g[part] + jnp.dot(rows, wg[slab], preferred_element_type=jnp.float32)
        u = acc_u[part] + jnp.dot(rows, wu[slab], preferred_element_type=jnp.float32)
        hid[part] = (v / (1.0 + jnp.exp(-v)) * u).astype(jnp.bfloat16)

    def produce_for(q, t):
        rows = pl.ds(pl.multiple_of(2 * level[t] * ROWS, 2 * ROWS), 2 * ROWS)
        part = pl.ds(pl.multiple_of(q * F, F), F)
        y = jnp.dot(hid[rows], wd[:, part], preferred_element_type=jnp.float32).astype(jnp.bfloat16)
        for g in (1, 0):
            so[q, level[t], g] = y[g * ROWS : (g + 1) * ROWS]

    def product(q):
        part = pl.ds(pl.multiple_of(q * F, F), F)
        return jnp.dot(hid[...], wd[:, part], preferred_element_type=jnp.float32).astype(jnp.bfloat16)

    def produce(q):
        y = product(q)
        for k in range(4):
            for g in range(2):
                n = (2 * k + g) * ROWS
                so[q, k, g] = y[n : n + ROWS]
        give(q, 1)
        give(q - 1, 0)

    def give(q, g):
        for t in (2, 3, 1):
            y_copy(q, t, g).start()
        y_own(q, g).start()

    def produce_e(i):
        y = product(E + i)
        for s in range(2):
            for j in range(2):
                for g in range(2):
                    n = ((2 * s + j) * 2 + g) * ROWS
                    so[E + i, 2 * j + s, g] = y[n : n + ROWS]
        ye_copy(i).start()
        ye_own(i).start()

    def unselect(g):
        def body(q):
            for t in (1, 2, 3):
                y_copy(q, t, g).wait_recv()
            y_own(q, g).wait()
            rows = yr[q, g].reshape(4 * ROWS, F)
            sums = jnp.dot(wmap[g], rows, preferred_element_type=jnp.float32)
            for i in range(GROUP):
                block = sums[i * tok : (i + 1) * tok]
                if g * GROUP + i == 7:
                    for way in (0, 1):
                        part = slice(way * half, (way + 1) * half)
                        xb[q, way * 4, part] = block[part].astype(jnp.bfloat16)
                else:
                    cb[q % KEPT, g * GROUP + i] = block
            if g == 1:
                for way in (0, 1):
                    rs_copy(q, way, 0).start()

        return body

    def unselect_e(i):
        ye_copy(i).wait_recv()
        ye_own(i).wait()
        for g in (1, 0):
            for col in (0, 1):
                source = 1 - a if col else a
                rows = yr_e[i, source, g].reshape(2 * ROWS, F)
                sums = jnp.dot(wmap_e[col, g], rows, preferred_element_type=jnp.float32)
                for n in range(GROUP):
                    block = sums[n * tok : (n + 1) * tok]
                    if g * GROUP + n == 7:
                        for way in (0, 1):
                            part = slice(way * half, (way + 1) * half)
                            xe[i, col, way * 4, part] = block[part].astype(jnp.bfloat16)
                    else:
                        cb_e[i, col, g * GROUP + n] = block
            if g == 1:
                for way in (0, 1):
                    rse_copy(i, way, 0).start()

    def step(own, came, sent_on, way, s):
        if s == 1:
            add, keep = slice(way * half, (way + 1) * half), slice((1 - way) * half, (2 - way) * half)
            sent_on[add] = (own[add] + came[add].astype(jnp.float32)).astype(jnp.bfloat16)
            sent_on[keep] = own[keep].astype(jnp.bfloat16)
        else:
            sent_on[...] = (own[...] + came[...].astype(jnp.float32)).astype(jnp.bfloat16)

    def pass_on(s):
        def body(q):
            for way in (0, 1):
                rs_copy(q, way, s - 1).wait_recv()
                slot = SLOT[(4 - s) * (1 - 2 * way)]
                step(cb.at[q % KEPT, slot], rsr.at[q, way, s - 1], xb.at[q, way * 4 + s], way, s)
                rs_copy(q, way, s).start()

        return body

    def pass_on_e(i, s):
        for way in (0, 1):
            rse_copy(i, way, s - 1).wait_recv()
            slot = SLOT[(4 - s) * (1 - 2 * way)]
            for col in (0, 1):
                step(cb_e.at[i, col, slot], rsr_e.at[i, way, s - 1, col], xe.at[i, col, way * 4 + s], way, s)
            rse_copy(i, way, s).start()

    def finish(q):
        for way in (0, 1):
            rs_copy(q, way, 3).wait_recv()
        part = pl.ds(pl.multiple_of(q * F, F), F)
        moe = cb[q % KEPT, 0] + rsr[q, 0, 3].astype(jnp.float32) + rsr[q, 1, 3].astype(jnp.float32)
        outs[q] = (tokens[:, part].astype(jnp.float32) + moe).astype(jnp.bfloat16)
        pipe_copy(q).start()

    def cross_e(i):
        for way in (0, 1):
            rse_copy(i, way, 3).wait_recv()
        for col in (0, 1):
            total = cb_e[i, col, 0] + rsr_e[i, 0, 3, col].astype(jnp.float32) + rsr_e[i, 1, 3, col].astype(jnp.float32)
            if col:
                last[i, 0] = total.astype(jnp.bfloat16)
            else:
                cb_e[i, 0, 0] = total
        late_copy(i).start()

    def finish_e(i):
        late_copy(i).wait_recv()
        moe = cb_e[i, 0, 0] + last[i, 1].astype(jnp.float32)
        part = pl.ds(pl.multiple_of((E + i) * F, F), F)
        outs[E + i] = (tokens[:, part].astype(jnp.float32) + moe).astype(jnp.bfloat16)
        pipe_copy(E + i).start()

    def each_e(body):
        def one(i, carry):
            body(i)
            return carry

        lax.fori_loop(0, NE, one, 0)

    sent(0, 0)
    for t in (2, 3, 1, 0):
        for g in (0, 1):
            if t:
                x_copy(E - 1, t, g).wait_recv()
            else:
                x_own(E - 1, g).wait()
        act(t)
        produce_for(0, t)
        if t:
            y_copy(0, t, 1).start()
        else:
            y_own(0, 1).start()
    lax.fori_loop(1, E, sent, 0)
    for i in range(NE):
        for way in (0, 1):
            for s in range(1, 5):
                ze_copy(i, way, s).wait_send()
        early_copy(i).wait_send()
        xe_copy(i).wait_send()

    produce(1)
    each_e(produce_e)
    each_e(unselect_e)
    LEAD = 3

    def span(tau, d, body):
        def one(q, carry):
            body(q)
            return carry

        high = jnp.where(tau == E - 2 + d, E, jnp.minimum(tau - d + 1, E - 1))
        lax.fori_loop(jnp.maximum(tau - d, 0), high, one, 0)

    def combine_tick(tau, carry):
        span(tau, 3, finish)
        span(tau, 2, pass_on(3))

        @pl.when((tau >= 1) & (tau < E))
        def _():
            pass_on(2)(tau - 1)

        valid(tau, pass_on(1))
        for s in (1, 2, 3):

            @pl.when(tau == s - 1)
            def _():
                each_e(lambda i: pass_on_e(i, s))

        @pl.when(tau == 3)
        def _():
            each_e(cross_e)

        @pl.when(tau == 5)
        def _():
            each_e(finish_e)

        valid(tau + 1, unselect(1))

        @pl.when(tau + LEAD < E)
        def _():
            produce(tau + LEAD)

        @pl.when(tau + LEAD == E)
        def _():
            give(E - 1, 0)

        valid(tau, unselect(0))

        @pl.when(tau == E - 1)
        def _():
            pass_on(2)(tau)

        return carry

    lax.fori_loop(-1, E + 2, combine_tick, 0)

    def drain(q, carry):
        for way in (0, 1):
            for s in range(4):
                rs_copy(q, way, s).wait_send()
        for g in (0, 1):
            for t in (1, 2, 3):
                y_copy(q, t, g).wait_send()
        pipe_copy(q).wait()
        return carry

    for kind in (0, 1):
        for d in pt_all:
            pt_copy(kind, d).wait_send()
        pt_share(kind).wait_send()

    def drain_e(i):
        for way in (0, 1):
            for s in range(4):
                rse_copy(i, way, s).wait_send()
        late_copy(i).wait_send()
        ye_copy(i).wait_send()
        pipe_copy(E + i).wait()

    each_e(drain_e)
    lax.fori_loop(0, E, drain, 0)


def local(tokens, routes, norm_gain, router_weight, w_gate, w_up, w_down):
    tok, width = tokens.shape[1:]
    ff = w_gate.shape[3]
    nq = 8
    F = width // nq
    bf, f32 = jnp.bfloat16, jnp.float32
    vmem = pl.BlockSpec(memory_space=pltpu.VMEM)
    anywhere = pl.BlockSpec(memory_space=pl.ANY)
    dma = pltpu.SemaphoreType.DMA
    return pl.pallas_call(
        functools.partial(kernel, nq),
        out_shape=jax.ShapeDtypeStruct(tokens.shape, bf),
        in_specs=[anywhere, vmem, vmem, vmem, anywhere, anywhere, anywhere],
        out_specs=anywhere,
        scratch_shapes=[
            pltpu.VMEM((tok, width), bf),
            pltpu.VMEM((nq - NE, NZ, tok, F), bf),
            pltpu.VMEM((NE, 2, NZ, tok, F), bf),
            pltpu.VMEM((NZ, 16, tok), bf),
            pltpu.VMEM((NZ, 16, tok), bf),
            pltpu.VMEM((2, NZ, 16, tok), bf),
            pltpu.VMEM((2, NZ, 16, tok), bf),
            pltpu.VMEM((2, 4 * ROWS, GROUP * tok), bf),
            pltpu.VMEM((2, GROUP * tok, 4 * ROWS), bf),
            pltpu.VMEM((2, 2 * ROWS, GROUP * tok), bf),
            pltpu.VMEM((2, 2, GROUP * tok, 2 * ROWS), bf),
            pltpu.VMEM((nq, 4, 2, ROWS, F), bf),
            pltpu.VMEM((nq, 2, 2, 2, ROWS, F), bf),
            pltpu.VMEM((nq - NE, 2, 4, ROWS, F), bf),
            pltpu.VMEM((NE, 2, 2, 2, ROWS, F), bf),
            pltpu.VMEM((8 * ROWS, ff), f32),
            pltpu.VMEM((8 * ROWS, ff), f32),
            pltpu.VMEM((8 * ROWS, ff), bf),
            pltpu.VMEM((KEPT, 7, tok, F), f32),
            pltpu.VMEM((NE, 2, 7, tok, F), f32),
            pltpu.VMEM((nq - NE, 2, 4, tok, F), bf),
            pltpu.VMEM((NE, 2, 4, 2, tok, F), bf),
            pltpu.VMEM((NE, 2, tok, F), bf),
            pltpu.VMEM((nq, tok, F), bf),
            pltpu.VMEM((width, ff), bf),
            pltpu.VMEM((width, ff), bf),
            pltpu.VMEM((ff, width), bf),
            dma((nq, 2, 4)),
            dma((nq, 2, 4)),
            dma((2, 2, NZ)),
            dma((2, 2, NZ)),
            dma((nq, 4, 2)),
            dma((nq, 4, 2)),
            dma((nq, 4, 2)),
            dma((nq, 4, 2)),
            dma((nq, 2, 4)),
            dma((nq, 2, 4)),
            dma((NE, 2)),
            dma((NE, 2)),
            dma((nq,)),
            dma((nq,)),
            dma((4,)),
        ],
        compiler_params=pltpu.CompilerParams(
            collective_id=0, has_side_effects=True, vmem_limit_bytes=62 * 2**20
        ),
        name="relay_moe",
    )(tokens, jnp.transpose(routes, (2, 0, 1)), norm_gain, jnp.swapaxes(router_weight, 1, 2), w_gate, w_up, w_down)


def solution(mesh):
    return jax.shard_map(
        local,
        mesh=mesh,
        in_specs=(
            P("pipe", "expert", None),
            P("pipe", "expert", None),
            P("pipe", None),
            P("pipe", None, None),
            P("pipe", "expert", None, None),
            P("pipe", "expert", None, None),
            P("pipe", "expert", None, None),
        ),
        out_specs=P("pipe", "expert", None),
        check_vma=False,
    )
```

```python
import functools

import jax
import jax.numpy as jnp
from jax import lax
from jax.experimental import pallas as pl
from jax.experimental.pallas import tpu as pltpu
from jax.sharding import PartitionSpec as P

MESH = pl.DeviceIdType.MESH
NZ = 8
CAP = 36
GROUP = 4
ROWS = GROUP * CAP
NE = 1
KEPT = 4
FAR = 1024.0
SLOT = {0: 0, -1: 1, 1: 2, -2: 3, 2: 4, -3: 5, 3: 6, 4: 7, -4: 7}


def kernel(
    nq, tok_hbm, routes, gain, router, wg_hbm, wu_hbm, wd_hbm, out,
    tokens, xb, xe, own_rank, own_gate, pt_rank, pt_gate, sel, wmap, sel_e, wmap_e, so, xs, yr, yr_e, acc_g, acc_u, hid, cb, cb_e, rsr, rsr_e,
    last, outs, wg, wu, wd,
    zs_s, zs_r, pt_s, pt_r, xs_s, xs_r, ys_s, ys_r, rs_s, rs_r, ex_s, ex_r, pp_s, pp_r, w_sem,
):
    tok, width = tokens.shape
    tok_copy = pltpu.make_async_copy(tok_hbm.at[0], tokens, w_sem.at[3])
    tok_copy.start()
    half = tok // 2
    F = width // nq
    E = nq - NE
    p = lax.axis_index("pipe")
    e = lax.axis_index("expert")
    z, a, c = e // 4, (e // 2) % 2, e % 2
    mine = 2 * a + c

    def at_z(d):
        return {"expert": ((z + d + NZ) % NZ) * 4 + mine}

    level = [mine, 2 * a + (1 - c), 2 * (1 - a) + c, 2 * (1 - a) + (1 - c)]

    def at_level(t):
        return {"expert": z * 4 + level[t]}

    barrier = pltpu.get_barrier_semaphore()
    for d in range(1, NZ):
        pl.semaphore_signal(barrier, inc=1, device_id=at_z(d), device_id_type=MESH)
    for t in (1, 2, 3):
        pl.semaphore_signal(barrier, inc=1, device_id=at_level(t), device_id_type=MESH)
    pl.semaphore_signal(barrier, inc=1, device_id={"pipe": (p + 7) % 8}, device_id_type=MESH)

    w_copies = [
        pltpu.make_async_copy(wg_hbm.at[0, 0], wg, w_sem.at[0]),
        pltpu.make_async_copy(wu_hbm.at[0, 0], wu, w_sem.at[1]),
        pltpu.make_async_copy(wd_hbm.at[0, 0], wd, w_sem.at[2]),
    ]
    def remote(src, dst, s_sem, r_sem, where):
        return pltpu.make_async_remote_copy(
            src_ref=src, dst_ref=dst, send_sem=s_sem, recv_sem=r_sem, device_id=where, device_id_type=MESH
        )

    def z_copy(q, way, s):
        sign = 1 - 2 * way
        src, dst = xb.at[q, SLOT[-(s - 1) * sign]], xb.at[q, SLOT[-s * sign]]
        if s == 4:
            part = pl.ds(way * half, half)
            src, dst = src.at[part], dst.at[part]
        return remote(src, dst, zs_s.at[q, way, s - 1], zs_r.at[q, way, s - 1], at_z(sign))

    def ze_copy(i, way, s):
        sign = 1 - 2 * way
        src, dst = xe.at[i, :, SLOT[-(s - 1) * sign]], xe.at[i, :, SLOT[-s * sign]]
        if s == 4:
            part = pl.ds(way * half, half)
            src, dst = src.at[:, part], dst.at[:, part]
        return remote(src, dst, zs_s.at[E + i, way, s - 1], zs_r.at[E + i, way, s - 1], at_z(sign))

    def pt_copy(kind, d):
        n = SLOT[-d]
        mine_all, theirs = ((own_rank, pt_rank), (own_gate, pt_gate))[kind]
        return remote(
            mine_all.at[(z + d + NZ) % NZ], theirs.at[0, n], pt_s.at[kind, 0, n], pt_r.at[kind, 0, n], at_z(d)
        )

    def pt_share(kind):
        table = (pt_rank, pt_gate)[kind]
        return remote(table.at[0], table.at[1], pt_s.at[kind, 1, 0], pt_r.at[kind, 1, 0], at_level(2))

    pt_all = (1, -1, 2, -2, 3, -3, 4)

    def x_copy(q, t, g):
        return remote(
            so.at[q, level[t], g], xs.at[q, a, c, g], xs_s.at[q, t, g], xs_r.at[q, t, g], at_level(t)
        )

    def x_own(q, g):
        return pltpu.make_async_copy(so.at[q, mine, g], xs.at[q, a, c, g], xs_r.at[q, 0, g])

    def xe_copy(i):
        part = so.at[E + i, pl.ds(2 * (1 - c), 2)]
        return remote(part, xs.at[E + i, :, c], xs_s.at[E + i, 1, 0], xs_r.at[E + i, 1, 0], at_level(1))

    def xe_own(i):
        return pltpu.make_async_copy(so.at[E + i, pl.ds(2 * c, 2)], xs.at[E + i, :, c], xs_r.at[E + i, 0, 0])

    def y_copy(q, t, g):
        return remote(so.at[q, level[t], g], yr.at[q, g, mine], ys_s.at[q, t, g], ys_r.at[q, t, g], at_level(t))

    def y_own(q, g):
        return pltpu.make_async_copy(so.at[q, mine, g], yr.at[q, g, mine], ys_r.at[q, 0, g])

    def ye_copy(i):
        part = so.at[E + i, pl.ds(2 * (1 - c), 2)]
        return remote(part, yr_e.at[i, :, :, c], ys_s.at[E + i, 1, 0], ys_r.at[E + i, 1, 0], at_level(1))

    def ye_own(i):
        return pltpu.make_async_copy(so.at[E + i, pl.ds(2 * c, 2)], yr_e.at[i, :, :, c], ys_r.at[E + i, 0, 0])

    def early_copy(i):
        return remote(xe.at[i, 0, 0], xe.at[i, 1, 0], ex_s.at[i, 0], ex_r.at[i, 0], at_level(2))

    def late_copy(i):
        return remote(last.at[i, 0], last.at[i, 1], ex_s.at[i, 1], ex_r.at[i, 1], at_level(2))

    def rs_copy(q, way, s):
        sign = 1 - 2 * way
        src, dst = xb.at[q, way * 4 + s], rsr.at[q, way, s]
        if s == 0:
            part = pl.ds(way * half, half)
            src, dst = src.at[part], dst.at[part]
        return remote(src, dst, rs_s.at[q, way, s], rs_r.at[q, way, s], at_z(sign))

    def rse_copy(i, way, s):
        sign = 1 - 2 * way
        src, dst = xe.at[i, :, way * 4 + s], rsr_e.at[i, way, s]
        if s == 0:
            part = pl.ds(way * half, half)
            src, dst = src.at[:, part], dst.at[:, part]
        return remote(src, dst, rs_s.at[E + i, way, s], rs_r.at[E + i, way, s], at_z(sign))

    def pipe_copy(q):
        return remote(
            outs.at[q], out.at[0, :, pl.ds(pl.multiple_of(q * F, F), F)], pp_s.at[q], pp_r.at[q], {"pipe": (p + 1) % 8}
        )

    line = lax.broadcasted_iota(jnp.int32, (16 * NZ, 1), 0)
    expert_of = 4 * (line // 16) + line % 4
    hit = jnp.zeros((16 * NZ, tok), jnp.float32)
    for k in range(routes.shape[0]):
        hit = hit + (routes[k] == expert_of).astype(jnp.float32)
    later = (
        lax.broadcasted_iota(jnp.int32, (tok, tok), 0) < lax.broadcasted_iota(jnp.int32, (tok, tok), 1)
    ).astype(jnp.bfloat16)
    rank = jnp.dot(hit.astype(jnp.bfloat16), later, preferred_element_type=jnp.float32)
    own_rank[...] = jnp.where(hit > 0.0, rank, FAR).astype(jnp.bfloat16).reshape(NZ, 16, tok)
    pt_rank[0, 0] = own_rank[z]

    tok_copy.wait()
    wide = tokens[...].astype(jnp.float32)
    mean_square = jnp.mean(wide * wide, axis=-1, keepdims=True)
    normed = (wide * lax.rsqrt(mean_square + 1e-06) * gain[...]).astype(jnp.bfloat16)
    for q in range(E):
        xb[q, 0] = normed[:, q * F : (q + 1) * F]
    for i in range(NE):
        xe[i, 0, 0] = normed[:, (E + i) * F : (E + i + 1) * F]

    pl.semaphore_wait(barrier, 11)
    for way in (0, 1):
        z_copy(0, way, 1).start()
    for d in pt_all:
        pt_copy(0, d).start()
    for i in range(NE):
        early_copy(i).start()
    for w_copy in w_copies:
        w_copy.start()

    spread = (lax.broadcasted_iota(jnp.int32, (16 * NZ, router.shape[1]), 1) == expert_of).astype(jnp.bfloat16)
    tall_router = jnp.dot(spread, router[0], preferred_element_type=jnp.float32).astype(jnp.bfloat16)
    score = jax.nn.sigmoid(
        lax.dot_general(tall_router, normed, (((1,), (1,)), ((), ())), preferred_element_type=jnp.float32)
    )
    total = jnp.sum(jnp.where(line % 16 < 4, hit * score, 0.0), axis=0, keepdims=True)
    own_gate[...] = jnp.where(hit > 0.0, score / total, 0.0).astype(jnp.bfloat16).reshape(NZ, 16, tok)
    pt_gate[0, 0] = own_gate[z]

    def of_chip(first, second):
        return jnp.where(a == 0, first, second)

    def build_sel(g):
        for d in pt_all:
            if SLOT[-d] // GROUP == g:
                pt_copy(0, d).wait_recv()
        row = lax.broadcasted_iota(jnp.int32, (ROWS, tok), 0).astype(jnp.float32)
        for i in range(GROUP):
            tile = pt_rank[0, g * GROUP + i].astype(jnp.float32)
            for j in range(4):
                same = (row - float(CAP * i)) == tile[j : j + 1, :]
                sel[g, j * ROWS : (j + 1) * ROWS, i * tok : (i + 1) * tok] = jnp.where(same, 1.0, 0.0).astype(
                    jnp.bfloat16
                )

    def build_sel_e():
        pt_share(0).wait_recv()
        row = lax.broadcasted_iota(jnp.int32, (ROWS, tok), 0).astype(jnp.float32)
        for g in range(2):
            for i in range(GROUP):
                tile = pt_rank[1, g * GROUP + i].astype(jnp.float32)
                for j in range(2):
                    same = (row - float(CAP * i)) == of_chip(tile[j : j + 1, :], tile[2 + j : 3 + j, :])
                    sel_e[g, j * ROWS : (j + 1) * ROWS, i * tok : (i + 1) * tok] = jnp.where(same, 1.0, 0.0).astype(
                        jnp.bfloat16
                    )

    def build_wmap(col):
        if col == 0:
            for d in pt_all:
                pt_copy(1, d).wait_recv()
            pt_share(1).start()
        else:
            pt_share(1).wait_recv()
        turned, turned_gate = [
            jnp.transpose(table[col].reshape(16 * NZ, tok).astype(jnp.float32)) for table in (pt_rank, pt_gate)
        ]
        wide_place = lax.broadcasted_iota(jnp.int32, (tok, 4 * ROWS), 1).astype(jnp.float32)
        place = lax.broadcasted_iota(jnp.int32, (tok, 2 * ROWS), 1).astype(jnp.float32)
        for g in range(2):
            for i in range(GROUP):
                first = (g * GROUP + i) * 16
                rank_of = [turned[:, first + j : first + j + 1] for j in range(4)]
                gate_of = [turned_gate[:, first + j : first + j + 1] for j in range(4)]
                part = slice(i * tok, (i + 1) * tok)
                if col == 0:
                    value = jnp.zeros((tok, 4 * ROWS), jnp.float32)
                    for j in range(4):
                        value = jnp.where(wide_place == rank_of[j] + float(ROWS * j + CAP * i), gate_of[j], value)
                    wmap[g, part] = value.astype(jnp.bfloat16)
                value = jnp.zeros((tok, 2 * ROWS), jnp.float32)
                for j in range(2):
                    here = of_chip(rank_of[j], rank_of[2 + j]) + float(ROWS * j + CAP * i)
                    value = jnp.where(place == here, of_chip(gate_of[j], gate_of[2 + j]), value)
                wmap_e[col, g, part] = value.astype(jnp.bfloat16)

    def valid(q, body):
        @pl.when((q >= 0) & (q < E))
        def _():
            body(q)

    def forward(s):
        def body(q):
            for way in (0, 1):
                if s > 1:
                    z_copy(q, way, s - 1).wait_recv()
                z_copy(q, way, s).start()

        return body

    def forward_e(i, s):
        if s == 1:
            early_copy(i).wait_recv()
        for way in (0, 1):
            if s > 1:
                ze_copy(i, way, s - 1).wait_recv()
            ze_copy(i, way, s).start()

    def select(g):
        def body(q):
            if g == 1:
                for way in (0, 1):
                    z_copy(q, way, 4).wait_recv()
            block = xb[q, g * GROUP : (g + 1) * GROUP].reshape(GROUP * tok, F)
            picked = jnp.dot(sel[g], block, preferred_element_type=jnp.float32).astype(jnp.bfloat16)
            for j in range(4):
                so[q, j, g] = picked[j * ROWS : (j + 1) * ROWS]
            for t in (2, 3, 1):
                x_copy(q, t, g).start()
            x_own(q, g).start()

        return body

    def select_e(i):
        for way in (0, 1):
            ze_copy(i, way, 4).wait_recv()
        here = pl.ds(pl.multiple_of(a * 2 * ROWS, 2 * ROWS), 2 * ROWS)
        for g in range(2):
            for col in (0, 1):
                block = xe[i, col, g * GROUP : (g + 1) * GROUP].reshape(GROUP * tok, F)
                chosen = sel_e[g] if col else sel[g, here]
                picked = jnp.dot(chosen, block, preferred_element_type=jnp.float32).astype(jnp.bfloat16)
                source = 1 - a if col else a
                for j in range(2):
                    so[E + i, 2 * j + source, g] = picked[j * ROWS : (j + 1) * ROWS]
        xe_copy(i).start()
        xe_own(i).start()

    def multiply(q):
        rows = xs[q].reshape(8 * ROWS, F)
        part = pl.ds(pl.multiple_of(q * F, F), F)
        acc_g[...] += jnp.dot(rows, wg[part], preferred_element_type=jnp.float32)
        acc_u[...] += jnp.dot(rows, wu[part], preferred_element_type=jnp.float32)

    def receive(q):
        for g in (0, 1):
            for t in (1, 2, 3):
                x_copy(q, t, g).wait_recv()
            x_own(q, g).wait()

    def sent(q):
        for way in (0, 1):
            for s in range(1, 5):
                z_copy(q, way, s).wait_send()
        for g in (0, 1):
            for t in (1, 2, 3):
                x_copy(q, t, g).wait_send()

    LAG = 3

    def gather_tick(tau, carry):
        for s in (4, 3, 2, 1):
            if s > 1:
                valid(tau - s + 1, forward(s))
            else:

                @pl.when((tau > 0) & (tau < E))
                def _():
                    forward(1)(tau)

            @pl.when((tau - s + 1 >= E) & (tau - s + 1 < nq))
            def _():
                forward_e(tau - s + 1 - E, s)

            if s == 3:
                valid(tau - 2, select(0))

        valid(tau - 4, select(1))

        @pl.when((tau - 4 >= E) & (tau - 4 < nq))
        def _():
            select_e(tau - 4 - E)


        def take(q):
            receive(q)
            sent(q)
            multiply(q)

        @pl.when((tau - 4 - LAG >= 0) & (tau - 4 - LAG < E - 1))
        def _():
            take(tau - 4 - LAG)

        @pl.when((tau - 5 >= E) & (tau - 5 < nq))
        def _():
            xe_copy(tau - 5 - E).wait_recv()
            xe_own(tau - 5 - E).wait()
            multiply(tau - 5)

        return carry

    lax.fori_loop(1, 2, gather_tick, 0)
    build_sel(0)
    lax.fori_loop(2, 3, gather_tick, 0)
    build_sel(1)
    pt_share(0).start()
    lax.fori_loop(3, 5, gather_tick, 0)
    for d in pt_all:
        pt_copy(1, d).start()
    acc_g[...] = jnp.zeros_like(acc_g)
    acc_u[...] = jnp.zeros_like(acc_u)
    for w_copy in w_copies:
        w_copy.wait()
    lax.fori_loop(5, 7, gather_tick, 0)
    build_sel_e()
    lax.fori_loop(7, 8, gather_tick, 0)
    build_wmap(0)
    lax.fori_loop(8, 9, gather_tick, 0)
    build_wmap(1)
    lax.fori_loop(9, max(nq + 5, E + 3 + LAG), gather_tick, 0)

    sides = [(a, c), (a, 1 - c), (1 - a, c), (1 - a, 1 - c)]

    def act(t):
        part = pl.ds(pl.multiple_of(2 * level[t] * ROWS, 2 * ROWS), 2 * ROWS)
        rows = xs[(E - 1, *sides[t])].reshape(2 * ROWS, F)
        slab = slice((E - 1) * F, E * F)
        v = acc_g[part] + jnp.dot(rows, wg[slab], preferred_element_type=jnp.float32)
        u = acc_u[part] + jnp.dot(rows, wu[slab], preferred_element_type=jnp.float32)
        hid[part] = (v / (1.0 + jnp.exp(-v)) * u).astype(jnp.bfloat16)

    def produce_for(q, t):
        rows = pl.ds(pl.multiple_of(2 * level[t] * ROWS, 2 * ROWS), 2 * ROWS)
        part = pl.ds(pl.multiple_of(q * F, F), F)
        y = jnp.dot(hid[rows], wd[:, part], preferred_element_type=jnp.float32).astype(jnp.bfloat16)
        for g in (1, 0):
            so[q, level[t], g] = y[g * ROWS : (g + 1) * ROWS]

    def product(q):
        part = pl.ds(pl.multiple_of(q * F, F), F)
        return jnp.dot(hid[...], wd[:, part], preferred_element_type=jnp.float32).astype(jnp.bfloat16)

    def produce(q):
        y = product(q)
        for k in range(4):
            for g in range(2):
                n = (2 * k + g) * ROWS
                so[q, k, g] = y[n : n + ROWS]
        give(q, 1)
        give(q - 1, 0)

    def give(q, g):
        for t in (2, 3, 1):
            y_copy(q, t, g).start()
        y_own(q, g).start()

    def produce_e(i):
        y = product(E + i)
        for s in range(2):
            for j in range(2):
                for g in range(2):
                    n = ((2 * s + j) * 2 + g) * ROWS
                    so[E + i, 2 * j + s, g] = y[n : n + ROWS]
        ye_copy(i).start()
        ye_own(i).start()

    def unselect(g):
        def body(q):
            for t in (1, 2, 3):
                y_copy(q, t, g).wait_recv()
            y_own(q, g).wait()
            rows = yr[q, g].reshape(4 * ROWS, F)
            sums = jnp.dot(wmap[g], rows, preferred_element_type=jnp.float32)
            for i in range(GROUP):
                block = sums[i * tok : (i + 1) * tok]
                if g * GROUP + i == 7:
                    for way in (0, 1):
                        part = slice(way * half, (way + 1) * half)
                        xb[q, way * 4, part] = block[part].astype(jnp.bfloat16)
                else:
                    cb[q % KEPT, g * GROUP + i] = block
            if g == 1:
                for way in (0, 1):
                    rs_copy(q, way, 0).start()

        return body

    def unselect_e(i):
        ye_copy(i).wait_recv()
        ye_own(i).wait()
        for g in (1, 0):
            for col in (0, 1):
                source = 1 - a if col else a
                rows = yr_e[i, source, g].reshape(2 * ROWS, F)
                sums = jnp.dot(wmap_e[col, g], rows, preferred_element_type=jnp.float32)
                for n in range(GROUP):
                    block = sums[n * tok : (n + 1) * tok]
                    if g * GROUP + n == 7:
                        for way in (0, 1):
                            part = slice(way * half, (way + 1) * half)
                            xe[i, col, way * 4, part] = block[part].astype(jnp.bfloat16)
                    else:
                        cb_e[i, col, g * GROUP + n] = block
            if g == 1:
                for way in (0, 1):
                    rse_copy(i, way, 0).start()

    def step(own, came, sent_on, way, s):
        if s == 1:
            add, keep = slice(way * half, (way + 1) * half), slice((1 - way) * half, (2 - way) * half)
            sent_on[add] = (own[add] + came[add].astype(jnp.float32)).astype(jnp.bfloat16)
            sent_on[keep] = own[keep].astype(jnp.bfloat16)
        else:
            sent_on[...] = (own[...] + came[...].astype(jnp.float32)).astype(jnp.bfloat16)

    def pass_on(s):
        def body(q):
            for way in (0, 1):
                rs_copy(q, way, s - 1).wait_recv()
                slot = SLOT[(4 - s) * (1 - 2 * way)]
                step(cb.at[q % KEPT, slot], rsr.at[q, way, s - 1], xb.at[q, way * 4 + s], way, s)
                rs_copy(q, way, s).start()

        return body

    def pass_on_e(i, s):
        for way in (0, 1):
            rse_copy(i, way, s - 1).wait_recv()
            slot = SLOT[(4 - s) * (1 - 2 * way)]
            for col in (0, 1):
                step(cb_e.at[i, col, slot], rsr_e.at[i, way, s - 1, col], xe.at[i, col, way * 4 + s], way, s)
            rse_copy(i, way, s).start()

    def finish(q):
        for way in (0, 1):
            rs_copy(q, way, 3).wait_recv()
        part = pl.ds(pl.multiple_of(q * F, F), F)
        moe = cb[q % KEPT, 0] + rsr[q, 0, 3].astype(jnp.float32) + rsr[q, 1, 3].astype(jnp.float32)
        outs[q] = (tokens[:, part].astype(jnp.float32) + moe).astype(jnp.bfloat16)
        pipe_copy(q).start()

    def cross_e(i):
        for way in (0, 1):
            rse_copy(i, way, 3).wait_recv()
        for col in (0, 1):
            total = cb_e[i, col, 0] + rsr_e[i, 0, 3, col].astype(jnp.float32) + rsr_e[i, 1, 3, col].astype(jnp.float32)
            if col:
                last[i, 0] = total.astype(jnp.bfloat16)
            else:
                cb_e[i, 0, 0] = total
        late_copy(i).start()

    def finish_e(i):
        late_copy(i).wait_recv()
        moe = cb_e[i, 0, 0] + last[i, 1].astype(jnp.float32)
        part = pl.ds(pl.multiple_of((E + i) * F, F), F)
        outs[E + i] = (tokens[:, part].astype(jnp.float32) + moe).astype(jnp.bfloat16)
        pipe_copy(E + i).start()

    def each_e(body):
        def one(i, carry):
            body(i)
            return carry

        lax.fori_loop(0, NE, one, 0)

    for t in (2, 3, 1, 0):
        for g in (0, 1):
            if t:
                x_copy(E - 1, t, g).wait_recv()
            else:
                x_own(E - 1, g).wait()
        act(t)
        produce_for(0, t)
        if t:
            y_copy(0, t, 1).start()
        else:
            y_own(0, 1).start()
    sent(E - 1)
    for i in range(NE):
        for way in (0, 1):
            for s in range(1, 5):
                ze_copy(i, way, s).wait_send()
        early_copy(i).wait_send()
        xe_copy(i).wait_send()

    produce(1)
    each_e(produce_e)
    each_e(unselect_e)
    produce(2)
    LEAD = 4

    def span(tau, d, body):
        def one(q, carry):
            body(q)
            return carry

        high = jnp.where(tau == E - 2 + d, E, jnp.minimum(tau - d + 1, E - 1))
        lax.fori_loop(jnp.maximum(tau - d, 0), high, one, 0)

    def drain(q):
        for way in (0, 1):
            for s in range(4):
                rs_copy(q, way, s).wait_send()
        for g in (0, 1):
            for t in (1, 2, 3):
                y_copy(q, t, g).wait_send()
        pipe_copy(q).wait_send()

    def drain_e(i):
        for way in (0, 1):
            for s in range(4):
                rse_copy(i, way, s).wait_send()
        late_copy(i).wait_send()
        ye_copy(i).wait_send()
        pipe_copy(E + i).wait_send()

    def combine_tick(tau, carry):
        span(tau, 3, finish)
        span(tau, 2, pass_on(3))

        @pl.when((tau >= 1) & (tau < E))
        def _():
            pass_on(2)(tau - 1)

        valid(tau, pass_on(1))
        for s in (1, 2, 3):

            @pl.when(tau == s - 1)
            def _():
                each_e(lambda i: pass_on_e(i, s))

        @pl.when(tau == 3)
        def _():
            each_e(cross_e)

        @pl.when(tau == 5)
        def _():
            each_e(finish_e)

        valid(tau + 1, unselect(1))

        @pl.when(tau + LEAD < E)
        def _():
            produce(tau + LEAD)

        @pl.when(tau + LEAD == E)
        def _():
            give(E - 1, 0)

        valid(tau, unselect(0))

        @pl.when(tau == E - 1)
        def _():
            pass_on(2)(tau)

        @pl.when((tau >= 4) & (tau - 4 < E - 2))
        def _():
            drain(tau - 4)

        @pl.when(tau == 6)
        def _():
            each_e(drain_e)
            for kind in (0, 1):
                for d in pt_all:
                    pt_copy(kind, d).wait_send()
                pt_share(kind).wait_send()

        return carry

    lax.fori_loop(-1, E + 2, combine_tick, 0)

    for q in (E - 2, E - 1):
        drain(q)

    def arrive(q, carry):
        pipe_copy(q).wait_recv()
        return carry

    lax.fori_loop(0, nq, arrive, 0)


def local(tokens, routes, norm_gain, router_weight, w_gate, w_up, w_down):
    tok, width = tokens.shape[1:]
    ff = w_gate.shape[3]
    nq = 8
    F = width // nq
    bf, f32 = jnp.bfloat16, jnp.float32
    vmem = pl.BlockSpec(memory_space=pltpu.VMEM)
    anywhere = pl.BlockSpec(memory_space=pl.ANY)
    dma = pltpu.SemaphoreType.DMA
    return pl.pallas_call(
        functools.partial(kernel, nq),
        out_shape=jax.ShapeDtypeStruct(tokens.shape, bf),
        in_specs=[anywhere, vmem, vmem, vmem, anywhere, anywhere, anywhere],
        out_specs=anywhere,
        scratch_shapes=[
            pltpu.VMEM((tok, width), bf),
            pltpu.VMEM((nq - NE, NZ, tok, F), bf),
            pltpu.VMEM((NE, 2, NZ, tok, F), bf),
            pltpu.VMEM((NZ, 16, tok), bf),
            pltpu.VMEM((NZ, 16, tok), bf),
            pltpu.VMEM((2, NZ, 16, tok), bf),
            pltpu.VMEM((2, NZ, 16, tok), bf),
            pltpu.VMEM((2, 4 * ROWS, GROUP * tok), bf),
            pltpu.VMEM((2, GROUP * tok, 4 * ROWS), bf),
            pltpu.VMEM((2, 2 * ROWS, GROUP * tok), bf),
            pltpu.VMEM((2, 2, GROUP * tok, 2 * ROWS), bf),
            pltpu.VMEM((nq, 4, 2, ROWS, F), bf),
            pltpu.VMEM((nq, 2, 2, 2, ROWS, F), bf),
            pltpu.VMEM((nq - NE, 2, 4, ROWS, F), bf),
            pltpu.VMEM((NE, 2, 2, 2, ROWS, F), bf),
            pltpu.VMEM((8 * ROWS, ff), f32),
            pltpu.VMEM((8 * ROWS, ff), f32),
            pltpu.VMEM((8 * ROWS, ff), bf),
            pltpu.VMEM((KEPT, 7, tok, F), f32),
            pltpu.VMEM((NE, 2, 7, tok, F), f32),
            pltpu.VMEM((nq - NE, 2, 4, tok, F), bf),
            pltpu.VMEM((NE, 2, 4, 2, tok, F), bf),
            pltpu.VMEM((NE, 2, tok, F), bf),
            pltpu.VMEM((nq, tok, F), bf),
            pltpu.VMEM((width, ff), bf),
            pltpu.VMEM((width, ff), bf),
            pltpu.VMEM((ff, width), bf),
            dma((nq, 2, 4)),
            dma((nq, 2, 4)),
            dma((2, 2, NZ)),
            dma((2, 2, NZ)),
            dma((nq, 4, 2)),
            dma((nq, 4, 2)),
            dma((nq, 4, 2)),
            dma((nq, 4, 2)),
            dma((nq, 2, 4)),
            dma((nq, 2, 4)),
            dma((NE, 2)),
            dma((NE, 2)),
            dma((nq,)),
            dma((nq,)),
            dma((4,)),
        ],
        compiler_params=pltpu.CompilerParams(
            collective_id=0, has_side_effects=True, vmem_limit_bytes=62 * 2**20
        ),
        name="relay_moe",
    )(tokens, jnp.transpose(routes, (2, 0, 1)), norm_gain, jnp.swapaxes(router_weight, 1, 2), w_gate, w_up, w_down)


def solution(mesh):
    return jax.shard_map(
        local,
        mesh=mesh,
        in_specs=(
            P("pipe", "expert", None),
            P("pipe", "expert", None),
            P("pipe", None),
            P("pipe", None, None),
            P("pipe", "expert", None, None),
            P("pipe", "expert", None, None),
            P("pipe", "expert", None, None),
        ),
        out_specs=P("pipe", "expert", None),
        check_vma=False,
    )
```
